32 devices in a mesh: asset: 8 (over z, core), frame: 2 (over y), row: 2 (over x).
Axes of the slice: x: 2, y: 2, z: 4, core: 2. Of those that a mesh axis runs over, the one named last changes fastest.
Arguments:
- latent: bfloat16 [16, 4, 72, 1280], P(('asset', 'frame'), 'row'), parts along dimension 0, may hold values from -36 to 36
- timestep: int32 [8], P('asset'), parts along dimension 0, may hold values from 0 to 999
- camera: int32 [16, 2], P('asset'), parts along dimension 0, may hold values from 0 to 359
- dec_feat: bfloat16 [16, 4, 72, 512], P(('asset', 'frame'), 'row'), parts along dimension 0, may hold values from -36 to 36
- norm_gain: float32 [1280], replicated, may hold values from 0.1 to 1.9
- norm_shift: float32 [1280], replicated, may hold values from -3 to 3
- emb_weight: bfloat16 [960, 1280], replicated, may hold values from -0.375 to 0.375
- conv_weight: bfloat16 [3, 3, 1280, 1280], P(None, None, None, 'frame'), may hold values from -0.0546875 to 0.0546875
- ln_gain: float32 [1280], replicated, may hold values from 0.1 to 1.9
- q_weight: bfloat16 [1280, 1280], P(('frame', 'row')), may hold values from -0.15625 to 0.15625
- k_weight: bfloat16 [1280, 1280], P(('frame', 'row')), may hold values from -0.15625 to 0.15625
- v_weight: bfloat16 [1280, 1280], P(('frame', 'row')), may hold values from -0.15625 to 0.15625
- o_weight: bfloat16 [1280, 1280], P(('frame', 'row')), may hold values from -0.15625 to 0.15625
- dec_gain: float32 [512], replicated, may hold values from 0.1 to 1.9
- dec_shift: float32 [512], replicated, may hold values from -3 to 3
- time_weight: bfloat16 [3, 512, 512], replicated, may hold values from -0.15625 to 0.15625
Outputs:
- unet_out: bfloat16 [16, 4, 72, 1280], P(('asset', 'frame'), 'row'), parts along dimension 0
- dec_out: bfloat16 [16, 4, 72, 512], P(('asset', 'frame'), 'row'), parts along dimension 0
The draws below stay inside these ranges and needn't reach their ends.
There are 8 independent parts, one for each index of `asset`. The reference program is written for one: setup_inputs(seed, part) draws one part's arguments, and reference() takes and returns one part's arrays. A program takes and returns all parts, laid end to end along the dimension named above; an argument that names none is the same for every part. Nothing has to cross between parts.
All inputs are finite; a program needn't handle non-finite values.
Results may differ from the reference program's by a relative error of at most 0.0056.
Values may be sent and summed in bfloat16 or wider, within the bound.
A program may use at most 128 MiB of HBM per device.

```python
import math
import jax
import jax.numpy as jnp
from jax import lax

C = 1280
HEADS = 20
HD = 64
G = 32
EMB = 320
DC = 512
W = 72
FRAMES = 2
H = 4
DH = 4


def ramp_field(key, base, along, number):
    shape = base.shape
    keys = jax.random.split(key, 2)
    channel = jnp.power(10.0, jax.random.uniform(keys[0], (shape[-1],), jnp.float32) - 0.5)
    cell = jax.random.uniform(keys[1], shape[:-1] + (1,), jnp.float32, 0.6, 1.6)
    position = jnp.arange(shape[along], dtype=jnp.float32) / (number - 1)
    ramp = jnp.power(3.0, position - 0.5)
    ramp_shape = [1] * len(shape)
    ramp_shape[along] = shape[along]
    return base * channel * cell * ramp.reshape(ramp_shape)


def draw_latent(key, part):
    shape = (FRAMES, H, W, C)
    base_key = jax.random.fold_in(key, 11)
    base = jax.random.truncated_normal(base_key, -4.0, 4.0, shape, jnp.float32)
    return ramp_field(jax.random.fold_in(key, 12), base, 1, H).astype(jnp.bfloat16)


def draw_dec_feat(key, part):
    shape = (FRAMES, DH, W, DC)
    base_key = jax.random.fold_in(key, 21)
    base = jax.random.truncated_normal(base_key, -4.0, 4.0, shape, jnp.float32)
    return ramp_field(jax.random.fold_in(key, 22), base, 0, FRAMES).astype(jnp.bfloat16)


def plant(values, stream_key, smallest, high):
    longest = values.shape.index(max(values.shape))
    spots = []
    for shift in (0, 1):
        where = [jax.random.randint(jax.random.fold_in(stream_key, axis), (), 0, length) for axis, length in enumerate(values.shape)]
        where[longest] = (where[longest] + shift) % values.shape[longest]
        spots.append(tuple(where))
    return values.at[spots[0]].set(smallest).at[spots[1]].set(high)


def steps_of(rng, shape, cuts, low, high):
    level = 1.0
    for axis_at, shards_of in cuts:
        heights = jax.random.uniform(jax.random.fold_in(jax.random.fold_in(rng, 6), axis_at), (shards_of,), jnp.float32, low / len(cuts), high / len(cuts))
        level = level * jnp.repeat(jnp.exp(heights), shape[axis_at] // shards_of).reshape((-1,) + (1,) * (len(shape) - 1 - axis_at))
    return level


def centred(stream_key, shape, width, limit, cuts=(), kind=jnp.bfloat16):
    array = width * jax.random.normal(stream_key, shape, jnp.float32)
    if cuts:
        array = array * steps_of(stream_key, shape, cuts, -0.22, 0.18)
    return jnp.clip(array, -limit, limit).astype(kind)


def setup_inputs(seed: int = 0, part: int = 0) -> dict:
    key_list = jax.random.split(jax.random.key(seed), 17)
    part_splits = jax.random.split(jax.random.fold_in(key_list[16], part), 17)
    latent = draw_latent(jax.random.fold_in(jax.random.fold_in(key_list[16], part), 71), part)
    timestep = jax.random.randint(part_splits[1], (1,), 0, 1000).astype(jnp.int32)
    camera = plant(jax.random.randint(part_splits[2], (FRAMES, 2), 0, 360), jax.random.fold_in(part_splits[2], 1), 0, 359).astype(jnp.int32)
    dec_feat = draw_dec_feat(jax.random.fold_in(jax.random.fold_in(key_list[16], part), 71), part)
    norm_gain = jnp.clip(1.0 + 0.18 * jax.random.normal(key_list[4], (C,), jnp.float32), 0.1, 1.9)
    norm_shift = centred(key_list[5], (C,), 0.5, 3.0, (), jnp.float32)
    emb_weight = centred(key_list[6], (3 * EMB, C), (3 * EMB // 4) ** -0.5, 0.375)
    conv_weight = centred(key_list[7], (3, 3, C, C), (9 * C) ** -0.5, 0.0546875, ((3, 2),))
    ln_gain = jnp.clip(1.0 + 0.18 * jax.random.normal(key_list[8], (C,), jnp.float32), 0.1, 1.9)
    q_weight = centred(key_list[9], (C, C), C ** -0.5, 0.15625, ((0, 4),))
    k_weight = centred(key_list[10], (C, C), C ** -0.5, 0.15625, ((0, 4),))
    v_weight = centred(key_list[11], (C, C), C ** -0.5, 0.15625, ((0, 4),))
    o_weight = centred(key_list[12], (C, C), C ** -0.5, 0.15625, ((0, 4),))
    dec_gain = jnp.clip(1.0 + 0.18 * jax.random.normal(key_list[13], (DC,), jnp.float32), 0.1, 1.9)
    dec_shift = centred(key_list[14], (DC,), 0.5, 3.0, (), jnp.float32)
    time_weight = centred(key_list[15], (3, DC, DC), (3 * DC) ** -0.5, 0.15625)
    return dict(latent=latent, timestep=timestep, camera=camera, dec_feat=dec_feat, norm_gain=norm_gain, norm_shift=norm_shift, emb_weight=emb_weight, conv_weight=conv_weight, ln_gain=ln_gain, q_weight=q_weight, k_weight=k_weight, v_weight=v_weight, o_weight=o_weight, dec_gain=dec_gain, dec_shift=dec_shift, time_weight=time_weight)


EPSILON = 1e-05

def sinusoids(values, entries):
    half = entries // 2
    freqs = jnp.exp(-math.log(10000.0) * jnp.arange(half, dtype=jnp.float32) / half)
    angles = values.astype(jnp.float32)[..., None] * freqs
    return jnp.concatenate([jnp.cos(angles), jnp.sin(angles)], axis=-1)

def conditions(timestep, camera, frames, entries):
    times = jnp.broadcast_to(timestep.astype(jnp.float32), (frames,))
    pieces = [sinusoids(times, entries), sinusoids(camera[:, 0], entries), sinusoids(camera[:, 1], entries)]
    return jax.nn.silu(jnp.concatenate(pieces, axis=-1)).astype(jnp.bfloat16)

def reference(latent, timestep, camera, dec_feat, norm_gain, norm_shift, emb_weight, conv_weight, ln_gain, q_weight, k_weight, v_weight, o_weight, dec_gain, dec_shift, time_weight):
    features = conditions(timestep, camera, FRAMES, EMB)
    cond = jnp.dot(features, emb_weight, preferred_element_type=jnp.float32)
    values = latent.astype(jnp.float32)
    grouped = values.reshape(FRAMES, H, W, G, C // G)
    number = H * W * (C // G)
    means = lax.optimization_barrier(jnp.sum(grouped, axis=(1, 2, 4))) / number
    squares = lax.optimization_barrier(jnp.sum(grouped * grouped, axis=(1, 2, 4))) / number
    scales = lax.rsqrt(squares - means * means + EPSILON)
    normed = (grouped - means[:, None, None, :, None]) * scales[:, None, None, :, None]
    normed = normed.reshape(FRAMES, H, W, C) * norm_gain + norm_shift
    act = jax.nn.silu(normed).astype(jnp.bfloat16)
    padded = jnp.pad(act, ((0, 0), (1, 1), (1, 1), (0, 0)))
    conv = jnp.zeros((FRAMES * H * W, C), jnp.float32)
    for down in range(3):
        for side in range(3):
            window = padded[:, down:down + H, side:side + W, :].reshape(-1, C)
            conv = conv + jnp.dot(window, conv_weight[down, side], preferred_element_type=jnp.float32)
    spatial = (values + conv.reshape(FRAMES, H, W, C) + cond[:, None, None, :]).astype(jnp.bfloat16)
    tokens = spatial.astype(jnp.float32).reshape(FRAMES, H * W, C)
    token_mean = lax.optimization_barrier(jnp.mean(tokens, axis=-1, keepdims=True))
    token_square = lax.optimization_barrier(jnp.mean(tokens * tokens, axis=-1, keepdims=True))
    token_scale = lax.rsqrt(token_square - token_mean * token_mean + EPSILON)
    normal = ((tokens - token_mean) * token_scale * ln_gain).astype(jnp.bfloat16).reshape(-1, C)
    query_rows = jnp.dot(normal, q_weight, preferred_element_type=jnp.float32).astype(jnp.bfloat16)
    key_rows = jnp.dot(normal, k_weight, preferred_element_type=jnp.float32).astype(jnp.bfloat16)
    value_rows = jnp.dot(normal, v_weight, preferred_element_type=jnp.float32).astype(jnp.bfloat16)
    query_rows = query_rows.reshape(FRAMES, H * W, HEADS, HD).astype(jnp.float32)
    key_rows = key_rows.reshape(FRAMES, H * W, HEADS, HD).astype(jnp.float32)
    value_rows = value_rows.reshape(FRAMES, H * W, HEADS, HD).astype(jnp.float32)
    scores = jnp.einsum('fphd,gphd->phfg', query_rows, key_rows) * (1.0 / math.sqrt(HD))
    weights = jnp.exp(scores)
    probs = (weights / lax.optimization_barrier(jnp.sum(weights, axis=-1, keepdims=True))).astype(jnp.bfloat16)
    mixed = jnp.einsum('phfg,gphd->fphd', probs.astype(jnp.float32), value_rows).astype(jnp.bfloat16).reshape(-1, C)
    attended = jnp.dot(mixed, o_weight, preferred_element_type=jnp.float32)
    unet_out = (tokens.reshape(-1, C) + attended).astype(jnp.bfloat16).reshape(FRAMES, H, W, C)
    dec_values = dec_feat.astype(jnp.float32)
    dec_grouped = dec_values.reshape(FRAMES, DH, W, G, DC // G)
    dec_number = FRAMES * DH * W * (DC // G)
    dec_means = lax.optimization_barrier(jnp.sum(dec_grouped, axis=(0, 1, 2, 4))) / dec_number
    dec_squares = lax.optimization_barrier(jnp.sum(dec_grouped * dec_grouped, axis=(0, 1, 2, 4))) / dec_number
    dec_scales = lax.rsqrt(dec_squares - dec_means * dec_means + EPSILON)
    dec_normed = ((dec_grouped - dec_means[:, None]) * dec_scales[:, None]).reshape(FRAMES, DH, W, DC)
    dec_act = jax.nn.silu(dec_normed * dec_gain + dec_shift).astype(jnp.bfloat16)
    before = jnp.roll(dec_act, 1, axis=0).reshape(-1, DC)
    after = jnp.roll(dec_act, -1, axis=0).reshape(-1, DC)
    middle = dec_act.reshape(-1, DC)
    temporal = jnp.dot(before, time_weight[0], preferred_element_type=jnp.float32)
    temporal = temporal + jnp.dot(middle, time_weight[1], preferred_element_type=jnp.float32)
    temporal = temporal + jnp.dot(after, time_weight[2], preferred_element_type=jnp.float32)
    dec_out = (dec_values + temporal.reshape(FRAMES, DH, W, DC)).astype(jnp.bfloat16)
    return (unet_out, dec_out)
```

```python
import math

import jax
import jax.numpy as jnp
from jax import lax
from jax.experimental import pallas as pl
from jax.experimental.pallas import tpu as pltpu
from jax.sharding import PartitionSpec as P

HEADS = 20
G = 32


EPSILON = 1e-05


def extended(cells, sides, width):
    for axis, dim in sides:
        count = lax.axis_size(axis)
        ends = count - 1
        head = lax.slice_in_dim(cells, 0, width, axis=dim)
        tail = lax.slice_in_dim(cells, cells.shape[dim] - width, cells.shape[dim], axis=dim)
        cells = jnp.concatenate(
            [
                lax.ppermute(tail, axis, [(i, (i + 1) % count) for i in range(ends)]),
                cells,
                lax.ppermute(head, axis, [((i + 1) % count, i) for i in range(ends)]),
            ],
            axis=dim,
        )
    return cells


def from_behind(block, axis, distance):
    devices = range(lax.axis_size(axis))
    route = [((i - distance) % len(devices), i) for i in devices]
    return lax.ppermute(block, axis, route)


def sinusoids(values, entries):
    half = entries // 2
    freqs = jnp.exp(-math.log(10000.0) * jnp.arange(half, dtype=jnp.float32) / half)
    angles = values.astype(jnp.float32)[..., None] * freqs
    return jnp.concatenate([jnp.cos(angles), jnp.sin(angles)], axis=-1)


def conditions(timestep, camera, frames, entries):
    times = jnp.broadcast_to(timestep.astype(jnp.float32), (frames,))
    pieces = [
        sinusoids(times, entries),
        sinusoids(camera[:, 0], entries),
        sinusoids(camera[:, 1], entries),
    ]
    return jax.nn.silu(jnp.concatenate(pieces, axis=-1)).astype(jnp.bfloat16)


def convolve(kernel, piece):
    number, rimmed, width, channels = piece.shape
    band = rimmed - 2
    outputs = kernel.shape[3]
    widened = jnp.pad(piece, ((0, 0), (0, 0), (1, 1), (0, 0)))
    total = jnp.zeros((number * band * width, outputs), jnp.float32)
    for down in range(3):
        for side in range(3):
            window = widened[:, down : down + band, side : side + width, :].reshape(-1, channels)
            total = total + jnp.dot(window, kernel[down, side], preferred_element_type=jnp.float32)
    return total.reshape(number, band, width, outputs)


def body(
    latent,
    timestep,
    camera,
    dec_feat,
    norm_gain,
    norm_shift,
    emb_weight,
    conv_weight,
    ln_gain,
    q_weight,
    k_weight,
    v_weight,
    o_weight,
    dec_gain,
    dec_shift,
    time_weight,
):
    frame_count = lax.axis_size("frame")
    row_count = lax.axis_size("row")
    frame_index = lax.axis_index("frame")
    local_frames, band, width, channels = latent.shape
    share = conv_weight.shape[3]
    frames = local_frames * frame_count
    groups = G
    heads = HEADS
    head_size = channels // heads
    features = conditions(timestep, camera, frames, emb_weight.shape[0] // 3)
    share_start = frame_index * share
    emb_share = lax.dynamic_slice_in_dim(emb_weight, share_start, share, 1)
    cond_share = jnp.dot(features, emb_share, preferred_element_type=jnp.float32)
    values = latent.astype(jnp.float32)
    grouped = values.reshape(local_frames, band, width, groups, channels // groups)
    sums, squares = lax.psum(
        (jnp.sum(grouped, axis=(1, 2, 4)), jnp.sum(grouped * grouped, axis=(1, 2, 4))), "row"
    )
    number = band * row_count * width * (channels // groups)
    means = sums / number
    scales = lax.rsqrt(squares / number - means * means + EPSILON)
    normed = (grouped - means[:, None, None, :, None]) * scales[:, None, None, :, None]
    normed = normed.reshape(local_frames, band, width, channels) * norm_gain + norm_shift
    act = jax.nn.silu(normed).astype(jnp.bfloat16)
    residual = lax.all_to_all(latent, "frame", split_axis=3, concat_axis=0, tiled=True).astype(
        jnp.float32
    )
    rimmed = extended(act, (("row", 1),), 1)
    conv = convolve(conv_weight, lax.all_gather(rimmed, "frame", axis=0, tiled=True))
    spatial = (residual + conv + cond_share[:, None, None, :]).astype(jnp.bfloat16)
    columns = lax.all_to_all(
        spatial.reshape(frames, band * width, share),
        "frame",
        split_axis=1,
        concat_axis=2,
        tiled=True,
    )
    pixels = columns.shape[1]
    tokens = columns.astype(jnp.float32)
    token_mean = jnp.mean(tokens, axis=-1, keepdims=True)
    token_square = jnp.mean(tokens * tokens, axis=-1, keepdims=True)
    token_scale = lax.rsqrt(token_square - token_mean * token_mean + EPSILON)
    normal = (
        ((tokens - token_mean) * token_scale * ln_gain).astype(jnp.bfloat16).reshape(-1, channels)
    )
    pieces = (
        lax.all_gather(q_weight, ("frame", "row"), axis=0, tiled=True),
        lax.all_gather(k_weight, ("frame", "row"), axis=0, tiled=True),
        lax.all_gather(v_weight, ("frame", "row"), axis=0, tiled=True),
    )
    inputs = normal
    query_rows, key_rows, value_rows = tuple(
        (jnp.dot(inputs, weight_part, preferred_element_type=jnp.float32) for weight_part in pieces)
    )
    query_rows = query_rows.astype(jnp.bfloat16).reshape(frames, pixels, heads, head_size)
    key_rows = key_rows.astype(jnp.bfloat16).reshape(frames, pixels, heads, head_size)
    value_rows = value_rows.astype(jnp.bfloat16).reshape(frames, pixels, heads, head_size)
    scores = jnp.einsum(
        "fphd,gphd->phfg", query_rows, key_rows, preferred_element_type=jnp.float32
    ) * (1.0 / math.sqrt(head_size))
    weights = jnp.exp(scores)
    probs = (weights / jnp.sum(weights, axis=-1, keepdims=True)).astype(jnp.bfloat16)
    mixed = (
        jnp.einsum("phfg,gphd->fphd", probs, value_rows, preferred_element_type=jnp.float32)
        .astype(jnp.bfloat16)
        .reshape(-1, channels)
    )
    inputs = mixed
    attended = jnp.dot(
        inputs,
        lax.all_gather(o_weight, ("frame", "row"), axis=0, tiled=True),
        preferred_element_type=jnp.float32,
    )
    result = (
        (tokens.reshape(-1, channels) + attended)
        .astype(jnp.bfloat16)
        .reshape(frames, pixels, channels)
    )
    unet_out = lax.all_to_all(result, "frame", split_axis=0, concat_axis=1, tiled=True).reshape(
        local_frames, band, width, channels
    )
    dec_frames, dec_band, dec_width, dec_channels = dec_feat.shape
    dec_values = dec_feat.astype(jnp.float32)
    dec_grouped = dec_values.reshape(
        dec_frames, dec_band, dec_width, groups, dec_channels // groups
    )
    dec_sums, dec_squares = lax.psum(
        (
            jnp.sum(dec_grouped, axis=(0, 1, 2, 4)),
            jnp.sum(dec_grouped * dec_grouped, axis=(0, 1, 2, 4)),
        ),
        ("frame", "row"),
    )
    dec_number = (
        dec_frames * frame_count * dec_band * row_count * dec_width * (dec_channels // groups)
    )
    dec_means = dec_sums / dec_number
    dec_scales = lax.rsqrt(dec_squares / dec_number - dec_means * dec_means + EPSILON)
    dec_normed = ((dec_grouped - dec_means[:, None]) * dec_scales[:, None]).reshape(
        dec_frames, dec_band, dec_width, dec_channels
    )
    dec_act = jax.nn.silu(dec_normed * dec_gain + dec_shift).astype(jnp.bfloat16)
    earlier = from_behind(dec_act, "frame", 1)
    later = from_behind(dec_act, "frame", -1)
    before = jnp.concatenate([earlier, dec_act[:-1]], axis=0).reshape(-1, dec_channels)
    after = jnp.concatenate([dec_act[1:], later], axis=0).reshape(-1, dec_channels)
    middle = dec_act.reshape(-1, dec_channels)
    temporal = jnp.dot(before, time_weight[0], preferred_element_type=jnp.float32)
    temporal = temporal + jnp.dot(middle, time_weight[1], preferred_element_type=jnp.float32)
    temporal = temporal + jnp.dot(after, time_weight[2], preferred_element_type=jnp.float32)
    dec_out = (dec_values + temporal.reshape(dec_frames, dec_band, dec_width, dec_channels)).astype(
        jnp.bfloat16
    )
    return (unet_out, dec_out)


def silu(x):
    return x * jax.nn.sigmoid(x)


def group_matrix(channels, groups):
    size = channels // groups
    channel = lax.broadcasted_iota(jnp.int32, (channels, 128), 0)
    low = lax.broadcasted_iota(jnp.int32, (channels, 128), 1) * size
    return jnp.where((channel >= low) & (channel < low + size), 1.0, 0.0).astype(jnp.float32)


def group_norm_terms(sums, number, channels):
    member = group_matrix(channels, G)
    grouped = jnp.dot(
        sums, member, precision=lax.Precision.HIGHEST, preferred_element_type=jnp.float32
    )
    spread = lax.dot_general(
        grouped,
        member,
        (((1,), (1,)), ((), ())),
        precision=lax.Precision.HIGHEST,
        preferred_element_type=jnp.float32,
    )
    mean = spread[0:1] / number
    square = spread[1:2] / number
    return mean, lax.rsqrt(square - mean * mean + EPSILON)


CHUNKS = ((0, 256), (256, 256), (512, 128))


def kernel(
    latent_ref,
    dec_ref,
    feats_ref,
    gain_ref,
    shift_ref,
    ln_ref,
    dgain_ref,
    dshift_ref,
    emb_hbm,
    conv_hbm,
    wsend_hbm,
    o_hbm,
    time_hbm,
    out_ref,
    dec_out_ref,
    convw,
    emb,
    ow,
    timew,
    latbuf,
    xcat,
    spat,
    wg,
    decoth,
    stats,
    psend,
    precv,
    load_sem,
    lat_send,
    lat_recv,
    dec_send,
    dec_recv,
    st_send,
    st_recv,
    w_send,
    w_recv,
    fw_send,
    fw_recv,
    sp_send,
    sp_recv,
    rs_send,
    rs_recv,
):
    MESH = pl.DeviceIdType.MESH
    asset = lax.axis_index("asset")
    f = lax.axis_index("frame")
    r = lax.axis_index("row")
    core = asset % 2
    sibling = asset + 1 - 2 * core
    me = 2 * f + r
    _, band, width, channels = latent_ref.shape
    cells = band * width
    share = convw.shape[3]
    rows = ow.shape[0]
    half = rows // 2
    dec_channels = dec_ref.shape[3]
    stride = width + 8

    def peer(k):
        pf = 1 - f if k >= 2 else f
        pr = 1 - r if k % 2 else r
        return pf, pr

    def remote(src, dst, send, recv, k):
        pf, pr = peer(k)
        return pltpu.make_async_remote_copy(
            src_ref=src,
            dst_ref=dst,
            send_sem=send,
            recv_sem=recv,
            device_id=(asset, pf, pr),
            device_id_type=MESH,
        )

    loads = [
        pltpu.make_async_copy(emb_hbm.at[:, pl.ds(pl.multiple_of(f * share, 128), share)], emb, load_sem.at[0]),
        pltpu.make_async_copy(conv_hbm.at[0], convw.at[0], load_sem.at[1]),
        pltpu.make_async_copy(conv_hbm.at[1], convw.at[1], load_sem.at[2]),
        pltpu.make_async_copy(conv_hbm.at[2], convw.at[2], load_sem.at[3]),
        pltpu.make_async_copy(time_hbm, timew, load_sem.at[4]),
        pltpu.make_async_copy(o_hbm, ow, load_sem.at[5]),
        pltpu.make_async_copy(
            wsend_hbm.at[me], wg.at[:, pl.ds(pl.multiple_of(me * rows, 16), rows), :], load_sem.at[6]
        ),
    ]
    for load in loads:
        load.start()

    barrier = pltpu.get_barrier_semaphore()
    for k in (1, 2, 3):
        pf, pr = peer(k)
        pl.semaphore_signal(barrier, inc=1, device_id=(asset, pf, pr), device_id_type=MESH)
    pl.semaphore_signal(barrier, inc=1, device_id=(sibling, f, r), device_id_type=MESH)
    pl.semaphore_wait(barrier, 4)

    def latent_copy(k, slot):
        return remote(latent_ref.at[0], latbuf.at[slot], lat_send.at[k], lat_recv.at[k], k)

    local_latent = pltpu.make_async_copy(latent_ref.at[0], latbuf.at[r], load_sem.at[7])

    @pl.when(f == r)
    def _():
        latent_copy(2, r).start()
        local_latent.start()

    @pl.when(f != r)
    def _():
        latent_copy(3, r).start()
        latent_copy(1, r).start()

    dec_copy = remote(dec_ref.at[0], decoth, dec_send, dec_recv, 2)
    dec_copy.start()

    dec_own = dec_ref[0].astype(jnp.float32).reshape(cells, dec_channels)
    dec_sum = jnp.sum(dec_own, axis=0, keepdims=True)
    dec_square = jnp.sum(dec_own * dec_own, axis=0, keepdims=True)
    stats[0] = jnp.concatenate(
        [dec_sum, dec_square, jnp.zeros((6, dec_channels), jnp.float32)], axis=0
    )
    stat_copies = [
        remote(stats.at[0], stats.at[k], st_send.at[k], st_recv.at[k], k) for k in (1, 2, 3)
    ]
    for copy in stat_copies:
        copy.start()

    loads[0].wait()
    cond = jnp.dot(feats_ref[...], emb[...], preferred_element_type=jnp.float32)[0:1]

    xcat[0:stride, :] = jnp.zeros((stride, 3 * channels), jnp.bfloat16)
    xcat[5 * stride : 6 * stride, :] = jnp.zeros((stride, 3 * channels), jnp.bfloat16)

    @pl.when(f == r)
    def _():
        local_latent.wait()
        latent_copy(1, 1 - r).wait_recv()

    @pl.when(f != r)
    def _():
        latent_copy(2, r).wait_recv()
        latent_copy(3, 1 - r).wait_recv()

    def weight_copy(k):
        pf, pr = peer(k)
        target = 2 * pf + pr
        mine = pl.ds(pl.multiple_of(core * half, 16), half)
        there = pl.ds(pl.multiple_of(me * rows + core * half, 16), half)
        return remote(
            wsend_hbm.at[target, :, mine, :], wg.at[:, there, :], w_send.at[k], w_recv.at[k], k
        )

    def weight_forward(k):
        pf, pr = peer(k)
        source = 2 * pf + pr
        piece = pl.ds(pl.multiple_of(source * rows + core * half, 16), half)
        return pltpu.make_async_remote_copy(
            src_ref=wg.at[:, piece, :],
            dst_ref=wg.at[:, piece, :],
            send_sem=fw_send.at[k],
            recv_sem=fw_recv.at[k],
            device_id=(sibling, f, r),
            device_id_type=MESH,
        )

    def weight_arrival(k, which):
        pf, pr = peer(k)
        source = 2 * pf + pr
        part = core if which == 0 else 1 - core
        piece = pl.ds(pl.multiple_of(source * rows + part * half, 16), half)
        sems = (w_send, w_recv) if which == 0 else (fw_send, fw_recv)
        return remote(wg.at[:, piece, :], wg.at[:, piece, :], sems[0].at[k], sems[1].at[k], k)

    for k in (3, 1, 2):
        weight_copy(k).start()

    total = jnp.zeros((1, channels), jnp.float32)
    square = jnp.zeros((1, channels), jnp.float32)
    for i in range(2 * band):
        x = latbuf[i // band, i % band].astype(jnp.float32)
        total = total + jnp.sum(x, axis=0, keepdims=True)
        square = square + jnp.sum(x * x, axis=0, keepdims=True)
    sums = jnp.concatenate([total, square, jnp.zeros((6, channels), jnp.float32)], axis=0)
    number = float(2 * cells * (channels // G))
    mean, scale = group_norm_terms(sums, number, channels)
    for i in range(2 * band):
        x = latbuf[i // band, i % band].astype(jnp.float32)
        act = silu((x - mean) * scale * gain_ref[...] + shift_ref[...])
        padded = jnp.concatenate([act, jnp.zeros((8, channels), jnp.float32)], axis=0)
        at = slice((i + 1) * stride, (i + 2) * stride)
        xcat[at, 0:channels] = pltpu.roll(padded, 1, 0).astype(jnp.bfloat16)
        xcat[at, channels : 2 * channels] = padded.astype(jnp.bfloat16)
        xcat[at, 2 * channels :] = pltpu.roll(padded, stride - 1, 0).astype(jnp.bfloat16)

    def spatial_copy(k, n, frame, start, size):
        where = spat.at[frame, :, pl.ds(pl.multiple_of(start, 128), size)]
        return remote(where, where, sp_send.at[n, k], sp_recv.at[n, k], k)

    for load in loads[1:4]:
        load.wait()
    for n, (start, size) in enumerate(CHUNKS):

        def tap(a, acc):
            lhs = xcat[pl.ds(pl.multiple_of(a * stride, 16), 2 * band * stride), :]
            rhs = convw[a, :, :, start : start + size].reshape(3 * channels, size)
            return acc + jnp.dot(lhs, rhs, preferred_element_type=jnp.float32)

        acc = lax.fori_loop(0, 3, tap, jnp.zeros((2 * band * stride, size), jnp.float32))
        acc = acc.reshape(2 * band, stride, size)[:, :width]
        column = pl.ds(pl.multiple_of(f * share + start, 128), size)
        res = latbuf[:, :, :, column].astype(jnp.float32).reshape(2 * band, width, size)
        new = res + acc + cond[:, start : start + size].reshape(1, 1, size)
        spat[r, :, column] = new.reshape(2 * cells, size).astype(jnp.bfloat16)
        for k in (3, 1, 2):
            spatial_copy(k, n, r, f * share + start, size).start()
        if n == 1:
            for k in (3, 1, 2):
                weight_arrival(k, 0).wait_recv()
                weight_forward(k).start()

    dec_copy.wait_recv()
    for copy in stat_copies:
        copy.wait_recv()
    dec_total = stats[0] + stats[1] + stats[2] + stats[3]
    dec_number = float(4 * cells * (dec_channels // G))
    dmean, dscale = group_norm_terms(dec_total, dec_number, dec_channels)

    def dec_act(x):
        return silu((x - dmean) * dscale * dgain_ref[...] + dshift_ref[...]).astype(jnp.bfloat16)

    dec_values = dec_ref[0].astype(jnp.float32).reshape(cells, dec_channels)
    middle = dec_act(dec_values)
    around = dec_act(decoth[...].astype(jnp.float32).reshape(cells, dec_channels))
    loads[4].wait()
    temporal = jnp.dot(around, timew[0], preferred_element_type=jnp.float32)
    temporal = temporal + jnp.dot(middle, timew[1], preferred_element_type=jnp.float32)
    temporal = temporal + jnp.dot(around, timew[2], preferred_element_type=jnp.float32)
    dec_out_ref[0] = (
        (dec_values + temporal).reshape(band, width, dec_channels).astype(jnp.bfloat16)
    )

    head_size = channels // HEADS
    lane = lax.broadcasted_iota(jnp.int32, (rows, 128), 0)
    low = lax.broadcasted_iota(jnp.int32, (rows, 128), 1) * head_size
    member = jnp.where((lane >= low) & (lane < low + head_size), 1.0, 0.0).astype(jnp.bfloat16)
    loads[5].wait()
    loads[6].wait()
    for n, (start, size) in enumerate(CHUNKS):
        for k in (1, 2, 3):
            pf, pr = peer(k)
            spatial_copy(k, n, pr, pf * share + start, size).wait_recv()
    for k in (3, 1, 2):
        weight_arrival(k, 1).wait_recv()

    def share_of(which):
        where = pl.ds(pl.multiple_of(which * cells, 16), cells)
        tokens = jnp.concatenate([spat[0, where, :], spat[1, where, :]], axis=0).astype(jnp.float32)
        mean = jnp.mean(tokens, axis=-1, keepdims=True)
        square = jnp.mean(tokens * tokens, axis=-1, keepdims=True)
        scale = lax.rsqrt(square - mean * mean + EPSILON)
        normal = ((tokens - mean) * scale * ln_ref[...]).astype(jnp.bfloat16)
        q, k, v = [
            jnp.dot(normal, wg[i], preferred_element_type=jnp.float32)
            .astype(jnp.bfloat16)
            .astype(jnp.float32)
            for i in range(3)
        ]
        high, rest = [], []
        for a in range(2):
            for b in range(2):
                product = q[a * cells : (a + 1) * cells] * k[b * cells : (b + 1) * cells]
                top = product.astype(jnp.bfloat16)
                high.append(top)
                rest.append((product - top.astype(jnp.float32)).astype(jnp.bfloat16))
        dots = jnp.dot(
            jnp.concatenate(high + rest, axis=0), member, preferred_element_type=jnp.float32
        )
        scores = (dots[: 4 * cells] + dots[4 * cells :]) * (1.0 / math.sqrt(head_size))
        weights = jnp.exp(scores)
        probs = []
        for a in range(2):
            pair = [weights[(2 * a + b) * cells : (2 * a + b + 1) * cells] for b in range(2)]
            bottom = pair[0] + pair[1]
            probs += [(one / bottom).astype(jnp.bfloat16) for one in pair]
        spread = lax.dot_general(
            jnp.concatenate(probs, axis=0),
            member,
            (((1,), (1,)), ((), ())),
            preferred_element_type=jnp.float32,
        )
        mixed = [
            spread[2 * a * cells : (2 * a + 1) * cells] * v[:cells]
            + spread[(2 * a + 1) * cells : (2 * a + 2) * cells] * v[cells:]
            for a in range(2)
        ]
        mixed = jnp.concatenate(mixed, axis=0).astype(jnp.bfloat16)
        return jnp.dot(mixed, ow[...], preferred_element_type=jnp.float32)

    def result_copy(k):
        return remote(psend.at[k], precv.at[k], rs_send.at[k], rs_recv.at[k], k)

    def tokens_of(frame):
        return pl.ds(pl.multiple_of(frame * cells, 8), cells)

    other = share_of(1 - r).astype(jnp.bfloat16)
    far = jnp.where(f == 0, other[cells:], other[:cells])
    near = jnp.where(f == 0, other[:cells], other[cells:])
    psend[3] = far
    result_copy(3).start()
    psend[1] = near
    result_copy(1).start()
    own = share_of(r)
    psend[2] = jnp.where(f == 0, own[cells:], own[:cells]).astype(jnp.bfloat16)
    result_copy(2).start()
    mine = jnp.where(f == 0, own[:cells], own[cells:])
    where = pl.ds(pl.multiple_of(r * cells, 16), cells)
    result = spat[f, where, :].astype(jnp.float32) + mine
    for k in (3, 1, 2):
        result_copy(k).wait_recv()
        result = result + precv[k].astype(jnp.float32)
    out_ref[0] = result.reshape(band, width, channels).astype(jnp.bfloat16)

    @pl.when(f == r)
    def _():
        latent_copy(2, r).wait_send()

    @pl.when(f != r)
    def _():
        latent_copy(3, r).wait_send()
        latent_copy(1, r).wait_send()

    dec_copy.wait_send()
    for copy in stat_copies:
        copy.wait_send()
    for k in (1, 2, 3):
        weight_copy(k).wait_send()
        weight_forward(k).wait_send()
        result_copy(k).wait_send()
        for n, (start, size) in enumerate(CHUNKS):
            spatial_copy(k, n, r, f * share + start, size).wait_send()


def fused(
    latent,
    timestep,
    camera,
    dec_feat,
    norm_gain,
    norm_shift,
    emb_weight,
    conv_weight,
    ln_gain,
    q_weight,
    k_weight,
    v_weight,
    o_weight,
    dec_gain,
    dec_shift,
    time_weight,
):
    _, band, width, channels = latent.shape
    share = conv_weight.shape[3]
    rows = q_weight.shape[0]
    cells = band * width
    dec_channels = dec_feat.shape[3]
    features = conditions(timestep, camera, 2, emb_weight.shape[0] // 3)
    feats = lax.dynamic_slice_in_dim(features, lax.axis_index("row"), 1, 0)
    feats = jnp.broadcast_to(feats, (16, feats.shape[1]))
    wsend = jnp.stack([q_weight, k_weight, v_weight]).reshape(3, rows, 4, rows)
    wsend = wsend.transpose(2, 0, 1, 3)
    vmem = pl.BlockSpec(memory_space=pltpu.VMEM)
    hbm = pl.BlockSpec(memory_space=pl.ANY)
    dma = pltpu.SemaphoreType.DMA
    bf16, f32 = jnp.bfloat16, jnp.float32
    return pl.pallas_call(
        kernel,
        out_shape=(
            jax.ShapeDtypeStruct(latent.shape, bf16),
            jax.ShapeDtypeStruct(dec_feat.shape, bf16),
        ),
        in_specs=[vmem] * 8 + [hbm] * 5,
        out_specs=(vmem, vmem),
        scratch_shapes=[
            pltpu.VMEM(conv_weight.shape, bf16),
            pltpu.VMEM((emb_weight.shape[0], share), bf16),
            pltpu.VMEM(o_weight.shape, bf16),
            pltpu.VMEM(time_weight.shape, bf16),
            pltpu.VMEM((2, band, width, channels), bf16),
            pltpu.VMEM((6 * (width + 8), 3 * channels), bf16),
            pltpu.VMEM((2, 2 * cells, channels), bf16),
            pltpu.VMEM((3, channels, rows), bf16),
            pltpu.VMEM((band, width, dec_channels), bf16),
            pltpu.VMEM((4, 8, dec_channels), f32),
            pltpu.VMEM((4, cells, channels), bf16),
            pltpu.VMEM((4, cells, channels), bf16),
            dma((8,)),
            dma((4,)),
            dma((4,)),
            dma,
            dma,
            dma((4,)),
            dma((4,)),
            dma((4,)),
            dma((4,)),
            dma((4,)),
            dma((4,)),
            dma((3, 4)),
            dma((3, 4)),
            dma((4,)),
            dma((4,)),
        ],
        compiler_params=pltpu.CompilerParams(
            collective_id=0, has_side_effects=True, vmem_limit_bytes=60 * 1024 * 1024
        ),
        name="denoise",
    )(
        latent,
        dec_feat,
        feats,
        norm_gain.reshape(1, -1),
        norm_shift.reshape(1, -1),
        ln_gain.reshape(1, -1),
        dec_gain.reshape(1, -1),
        dec_shift.reshape(1, -1),
        emb_weight,
        conv_weight,
        wsend,
        o_weight,
        time_weight,
    )


def solution(mesh):
    in_specs = (
        P(("asset", "frame"), "row", None, None),
        P("asset"),
        P("asset", None),
        P(("asset", "frame"), "row", None, None),
        P(),
        P(),
        P(),
        P(None, None, None, "frame"),
        P(),
        P(("frame", "row"), None),
        P(("frame", "row"), None),
        P(("frame", "row"), None),
        P(("frame", "row"), None),
        P(),
        P(),
        P(),
    )
    out_specs = (P(("asset", "frame"), "row", None, None), P(("asset", "frame"), "row", None, None))
    sizes = dict(mesh.shape)
    small = sizes["frame"] == 2 and sizes["row"] == 2 and sizes["asset"] % 2 == 0
    return jax.shard_map(fused if small else body, mesh=mesh, in_specs=in_specs, out_specs=out_specs, check_vma=False)
```

```python
import math

import jax
import jax.numpy as jnp
from jax import lax
from jax.experimental import pallas as pl
from jax.experimental.pallas import tpu as pltpu
from jax.sharding import PartitionSpec as P

HEADS = 20
G = 32


EPSILON = 1e-05


def extended(cells, sides, width):
    for axis, dim in sides:
        count = lax.axis_size(axis)
        ends = count - 1
        head = lax.slice_in_dim(cells, 0, width, axis=dim)
        tail = lax.slice_in_dim(cells, cells.shape[dim] - width, cells.shape[dim], axis=dim)
        cells = jnp.concatenate(
            [
                lax.ppermute(tail, axis, [(i, (i + 1) % count) for i in range(ends)]),
                cells,
                lax.ppermute(head, axis, [((i + 1) % count, i) for i in range(ends)]),
            ],
            axis=dim,
        )
    return cells


def from_behind(block, axis, distance):
    devices = range(lax.axis_size(axis))
    route = [((i - distance) % len(devices), i) for i in devices]
    return lax.ppermute(block, axis, route)


def sinusoids(values, entries):
    half = entries // 2
    freqs = jnp.exp(-math.log(10000.0) * jnp.arange(half, dtype=jnp.float32) / half)
    angles = values.astype(jnp.float32)[..., None] * freqs
    return jnp.concatenate([jnp.cos(angles), jnp.sin(angles)], axis=-1)


def conditions(timestep, camera, frames, entries):
    times = jnp.broadcast_to(timestep.astype(jnp.float32), (frames,))
    pieces = [
        sinusoids(times, entries),
        sinusoids(camera[:, 0], entries),
        sinusoids(camera[:, 1], entries),
    ]
    return jax.nn.silu(jnp.concatenate(pieces, axis=-1)).astype(jnp.bfloat16)


def convolve(kernel, piece):
    number, rimmed, width, channels = piece.shape
    band = rimmed - 2
    outputs = kernel.shape[3]
    widened = jnp.pad(piece, ((0, 0), (0, 0), (1, 1), (0, 0)))
    total = jnp.zeros((number * band * width, outputs), jnp.float32)
    for down in range(3):
        for side in range(3):
            window = widened[:, down : down + band, side : side + width, :].reshape(-1, channels)
            total = total + jnp.dot(window, kernel[down, side], preferred_element_type=jnp.float32)
    return total.reshape(number, band, width, outputs)


def body(
    latent,
    timestep,
    camera,
    dec_feat,
    norm_gain,
    norm_shift,
    emb_weight,
    conv_weight,
    ln_gain,
    q_weight,
    k_weight,
    v_weight,
    o_weight,
    dec_gain,
    dec_shift,
    time_weight,
):
    frame_count = lax.axis_size("frame")
    row_count = lax.axis_size("row")
    frame_index = lax.axis_index("frame")
    local_frames, band, width, channels = latent.shape
    share = conv_weight.shape[3]
    frames = local_frames * frame_count
    groups = G
    heads = HEADS
    head_size = channels // heads
    features = conditions(timestep, camera, frames, emb_weight.shape[0] // 3)
    share_start = frame_index * share
    emb_share = lax.dynamic_slice_in_dim(emb_weight, share_start, share, 1)
    cond_share = jnp.dot(features, emb_share, preferred_element_type=jnp.float32)
    values = latent.astype(jnp.float32)
    grouped = values.reshape(local_frames, band, width, groups, channels // groups)
    sums, squares = lax.psum(
        (jnp.sum(grouped, axis=(1, 2, 4)), jnp.sum(grouped * grouped, axis=(1, 2, 4))), "row"
    )
    number = band * row_count * width * (channels // groups)
    means = sums / number
    scales = lax.rsqrt(squares / number - means * means + EPSILON)
    normed = (grouped - means[:, None, None, :, None]) * scales[:, None, None, :, None]
    normed = normed.reshape(local_frames, band, width, channels) * norm_gain + norm_shift
    act = jax.nn.silu(normed).astype(jnp.bfloat16)
    residual = lax.all_to_all(latent, "frame", split_axis=3, concat_axis=0, tiled=True).astype(
        jnp.float32
    )
    rimmed = extended(act, (("row", 1),), 1)
    conv = convolve(conv_weight, lax.all_gather(rimmed, "frame", axis=0, tiled=True))
    spatial = (residual + conv + cond_share[:, None, None, :]).astype(jnp.bfloat16)
    columns = lax.all_to_all(
        spatial.reshape(frames, band * width, share),
        "frame",
        split_axis=1,
        concat_axis=2,
        tiled=True,
    )
    pixels = columns.shape[1]
    tokens = columns.astype(jnp.float32)
    token_mean = jnp.mean(tokens, axis=-1, keepdims=True)
    token_square = jnp.mean(tokens * tokens, axis=-1, keepdims=True)
    token_scale = lax.rsqrt(token_square - token_mean * token_mean + EPSILON)
    normal = (
        ((tokens - token_mean) * token_scale * ln_gain).astype(jnp.bfloat16).reshape(-1, channels)
    )
    pieces = (
        lax.all_gather(q_weight, ("frame", "row"), axis=0, tiled=True),
        lax.all_gather(k_weight, ("frame", "row"), axis=0, tiled=True),
        lax.all_gather(v_weight, ("frame", "row"), axis=0, tiled=True),
    )
    inputs = normal
    query_rows, key_rows, value_rows = tuple(
        (jnp.dot(inputs, weight_part, preferred_element_type=jnp.float32) for weight_part in pieces)
    )
    query_rows = query_rows.astype(jnp.bfloat16).reshape(frames, pixels, heads, head_size)
    key_rows = key_rows.astype(jnp.bfloat16).reshape(frames, pixels, heads, head_size)
    value_rows = value_rows.astype(jnp.bfloat16).reshape(frames, pixels, heads, head_size)
    scores = jnp.einsum(
        "fphd,gphd->phfg", query_rows, key_rows, preferred_element_type=jnp.float32
    ) * (1.0 / math.sqrt(head_size))
    weights = jnp.exp(scores)
    probs = (weights / jnp.sum(weights, axis=-1, keepdims=True)).astype(jnp.bfloat16)
    mixed = (
        jnp.einsum("phfg,gphd->fphd", probs, value_rows, preferred_element_type=jnp.float32)
        .astype(jnp.bfloat16)
        .reshape(-1, channels)
    )
    inputs = mixed
    attended = jnp.dot(
        inputs,
        lax.all_gather(o_weight, ("frame", "row"), axis=0, tiled=True),
        preferred_element_type=jnp.float32,
    )
    result = (
        (tokens.reshape(-1, channels) + attended)
        .astype(jnp.bfloat16)
        .reshape(frames, pixels, channels)
    )
    unet_out = lax.all_to_all(result, "frame", split_axis=0, concat_axis=1, tiled=True).reshape(
        local_frames, band, width, channels
    )
    dec_frames, dec_band, dec_width, dec_channels = dec_feat.shape
    dec_values = dec_feat.astype(jnp.float32)
    dec_grouped = dec_values.reshape(
        dec_frames, dec_band, dec_width, groups, dec_channels // groups
    )
    dec_sums, dec_squares = lax.psum(
        (
            jnp.sum(dec_grouped, axis=(0, 1, 2, 4)),
            jnp.sum(dec_grouped * dec_grouped, axis=(0, 1, 2, 4)),
        ),
        ("frame", "row"),
    )
    dec_number = (
        dec_frames * frame_count * dec_band * row_count * dec_width * (dec_channels // groups)
    )
    dec_means = dec_sums / dec_number
    dec_scales = lax.rsqrt(dec_squares / dec_number - dec_means * dec_means + EPSILON)
    dec_normed = ((dec_grouped - dec_means[:, None]) * dec_scales[:, None]).reshape(
        dec_frames, dec_band, dec_width, dec_channels
    )
    dec_act = jax.nn.silu(dec_normed * dec_gain + dec_shift).astype(jnp.bfloat16)
    earlier = from_behind(dec_act, "frame", 1)
    later = from_behind(dec_act, "frame", -1)
    before = jnp.concatenate([earlier, dec_act[:-1]], axis=0).reshape(-1, dec_channels)
    after = jnp.concatenate([dec_act[1:], later], axis=0).reshape(-1, dec_channels)
    middle = dec_act.reshape(-1, dec_channels)
    temporal = jnp.dot(before, time_weight[0], preferred_element_type=jnp.float32)
    temporal = temporal + jnp.dot(middle, time_weight[1], preferred_element_type=jnp.float32)
    temporal = temporal + jnp.dot(after, time_weight[2], preferred_element_type=jnp.float32)
    dec_out = (dec_values + temporal.reshape(dec_frames, dec_band, dec_width, dec_channels)).astype(
        jnp.bfloat16
    )
    return (unet_out, dec_out)


def silu(x):
    return x * jax.nn.sigmoid(x)


def group_matrix(channels, groups):
    size = channels // groups
    channel = lax.broadcasted_iota(jnp.int32, (channels, 128), 0)
    low = lax.broadcasted_iota(jnp.int32, (channels, 128), 1) * size
    return jnp.where((channel >= low) & (channel < low + size), 1.0, 0.0).astype(jnp.float32)


def group_norm_terms(sums, number, channels):
    member = group_matrix(channels, G)
    grouped = jnp.dot(
        sums, member, precision=lax.Precision.HIGHEST, preferred_element_type=jnp.float32
    )
    spread = lax.dot_general(
        grouped,
        member,
        (((1,), (1,)), ((), ())),
        precision=lax.Precision.HIGHEST,
        preferred_element_type=jnp.float32,
    )
    mean = spread[0:1] / number
    square = spread[1:2] / number
    return mean, lax.rsqrt(square - mean * mean + EPSILON)


CHUNKS = ((0, 256), (256, 256), (512, 128))


def kernel(
    latent_ref,
    dec_ref,
    feats_ref,
    gain_ref,
    shift_ref,
    ln_ref,
    dgain_ref,
    dshift_ref,
    emb_hbm,
    conv_hbm,
    q_hbm,
    k_hbm,
    v_hbm,
    o_hbm,
    time_hbm,
    out_ref,
    dec_out_ref,
    wraw,
    wsend,
    relay,
    convw,
    emb,
    ow,
    timew,
    latbuf,
    xcat,
    spat,
    wg,
    decoth,
    stats,
    psend,
    precv,
    load_sem,
    lat_send,
    lat_recv,
    dec_send,
    dec_recv,
    st_send,
    st_recv,
    w_send,
    w_recv,
    zw_send,
    zw_recv,
    fw_send,
    fw_recv,
    rl_send,
    rl_recv,
    sp_send,
    sp_recv,
    rs_send,
    rs_recv,
):
    MESH = pl.DeviceIdType.MESH
    asset = lax.axis_index("asset")
    f = lax.axis_index("frame")
    r = lax.axis_index("row")
    core = asset % 2
    plane = asset // 2 % 2
    sibling = asset + 1 - 2 * core
    above = asset + 2 - 4 * plane
    me = 2 * f + r
    _, band, width, channels = latent_ref.shape
    cells = band * width
    share = convw.shape[3]
    rows = ow.shape[0]
    quarter = rows // 4
    part = 2 * plane + core
    part_above = 2 * (1 - plane) + core
    dec_channels = dec_ref.shape[3]
    stride = width + 8

    def peer(k):
        pf = 1 - f if k >= 2 else f
        pr = 1 - r if k % 2 else r
        return pf, pr

    def remote(src, dst, send, recv, k):
        pf, pr = peer(k)
        return pltpu.make_async_remote_copy(
            src_ref=src,
            dst_ref=dst,
            send_sem=send,
            recv_sem=recv,
            device_id=(asset, pf, pr),
            device_id_type=MESH,
        )

    raw = [
        pltpu.make_async_copy(ref, wraw.at[i], load_sem.at[8 + i])
        for i, ref in enumerate((q_hbm, k_hbm, v_hbm))
    ]
    for load in raw:
        load.start()
    loads = [
        pltpu.make_async_copy(
            emb_hbm.at[:, pl.ds(pl.multiple_of(f * share, 128), share)], emb, load_sem.at[0]
        ),
        pltpu.make_async_copy(conv_hbm.at[0], convw.at[0], load_sem.at[1]),
        pltpu.make_async_copy(conv_hbm.at[1], convw.at[1], load_sem.at[2]),
        pltpu.make_async_copy(conv_hbm.at[2], convw.at[2], load_sem.at[3]),
        pltpu.make_async_copy(time_hbm, timew, load_sem.at[4]),
        pltpu.make_async_copy(o_hbm, ow, load_sem.at[5]),
    ]
    for load in loads:
        load.start()

    barrier = pltpu.get_barrier_semaphore()
    for k in (1, 2, 3):
        pf, pr = peer(k)
        pl.semaphore_signal(barrier, inc=1, device_id=(asset, pf, pr), device_id_type=MESH)
    for other_asset in (sibling, above):
        pl.semaphore_signal(barrier, inc=1, device_id=(other_asset, f, r), device_id_type=MESH)
    pl.semaphore_wait(barrier, 5)

    def latent_copy(k, slot):
        return remote(latent_ref.at[0], latbuf.at[slot], lat_send.at[k], lat_recv.at[k], k)

    local_latent = pltpu.make_async_copy(latent_ref.at[0], latbuf.at[r], load_sem.at[7])

    def relay_copy(i):
        return remote(latent_ref.at[0, i], relay.at[i], rl_send.at[i], rl_recv.at[i], 2)

    def relay_forward(i, slot):
        return remote(relay.at[i], latbuf.at[slot, i], rl_send.at[i], rl_recv.at[i], 1)

    @pl.when(f == r)
    def _():
        latent_copy(2, r).start()
        local_latent.start()

    @pl.when(f != r)
    def _():
        for i in range(band):
            relay_copy(i).start()
        latent_copy(1, r).start()

    dec_copy = remote(dec_ref.at[0], decoth, dec_send, dec_recv, 2)
    dec_copy.start()

    dec_own = dec_ref[0].astype(jnp.float32).reshape(cells, dec_channels)
    dec_sum = jnp.sum(dec_own, axis=0, keepdims=True)
    dec_square = jnp.sum(dec_own * dec_own, axis=0, keepdims=True)
    stats[0] = jnp.concatenate(
        [dec_sum, dec_square, jnp.zeros((6, dec_channels), jnp.float32)], axis=0
    )
    stat_copies = [
        remote(stats.at[0], stats.at[k], st_send.at[k], st_recv.at[k], k) for k in (1, 2, 3)
    ]
    for copy in stat_copies:
        copy.start()

    for load in raw:
        load.wait()
    for i in range(3):
        for target in range(4):
            wsend[target, i] = wraw[i, :, target * rows : (target + 1) * rows]
    local_weight = pltpu.make_async_copy(
        wsend.at[me], wg.at[:, pl.ds(pl.multiple_of(me * rows, 16), rows), :], load_sem.at[6]
    )
    local_weight.start()

    loads[0].wait()
    cond = jnp.dot(feats_ref[...], emb[...], preferred_element_type=jnp.float32)[0:1]

    xcat[0:stride, :] = jnp.zeros((stride, 3 * channels), jnp.bfloat16)
    xcat[5 * stride : 6 * stride, :] = jnp.zeros((stride, 3 * channels), jnp.bfloat16)

    @pl.when(f == r)
    def _():
        local_latent.wait()
        for i in range(band):
            relay_copy(i).wait_recv()
            relay_forward(i, r).start()
        latent_copy(1, 1 - r).wait_recv()

    @pl.when(f != r)
    def _():
        latent_copy(2, r).wait_recv()
        for i in range(band):
            relay_forward(i, 1 - r).wait_recv()

    def source_rows(k, which):
        pf, pr = peer(k)
        source = 2 * pf + pr
        return pl.ds(pl.multiple_of(source * rows + which * quarter, 16), quarter)

    def weight_copy(k):
        pf, pr = peer(k)
        target = 2 * pf + pr
        mine = pl.ds(pl.multiple_of(part * quarter, 16), quarter)
        there = pl.ds(pl.multiple_of(me * rows + part * quarter, 16), quarter)
        return remote(
            wsend.at[target, :, mine, :], wg.at[:, there, :], w_send.at[k], w_recv.at[k], k
        )

    def weight_arrival(k):
        where = wg.at[:, source_rows(k, part), :]
        return remote(where, where, w_send.at[k], w_recv.at[k], k)

    def weight_pass(k, which, send, recv, other_asset):
        where = wg.at[:, source_rows(k, which), :]
        return pltpu.make_async_remote_copy(
            src_ref=where,
            dst_ref=where,
            send_sem=send,
            recv_sem=recv,
            device_id=(other_asset, f, r),
            device_id_type=MESH,
        )

    def weight_up(k, which):
        return weight_pass(k, which, zw_send.at[k], zw_recv.at[k], above)

    def weight_side(k, j, which):
        return weight_pass(k, which, fw_send.at[j, k], fw_recv.at[j, k], sibling)

    for k in (3, 1, 2):
        weight_copy(k).start()

    total = jnp.zeros((1, channels), jnp.float32)
    square = jnp.zeros((1, channels), jnp.float32)
    for i in range(2 * band):
        x = latbuf[i // band, i % band].astype(jnp.float32)
        total = total + jnp.sum(x, axis=0, keepdims=True)
        square = square + jnp.sum(x * x, axis=0, keepdims=True)
    sums = jnp.concatenate([total, square, jnp.zeros((6, channels), jnp.float32)], axis=0)
    number = float(2 * cells * (channels // G))
    mean, scale = group_norm_terms(sums, number, channels)
    for i in range(2 * band):
        x = latbuf[i // band, i % band].astype(jnp.float32)
        act = silu((x - mean) * scale * gain_ref[...].reshape(1, -1) + shift_ref[...].reshape(1, -1))
        padded = jnp.concatenate([act, jnp.zeros((8, channels), jnp.float32)], axis=0)
        at = slice((i + 1) * stride, (i + 2) * stride)
        xcat[at, 0:channels] = pltpu.roll(padded, 1, 0).astype(jnp.bfloat16)
        xcat[at, channels : 2 * channels] = padded.astype(jnp.bfloat16)
        xcat[at, 2 * channels :] = pltpu.roll(padded, stride - 1, 0).astype(jnp.bfloat16)

    def spatial_copy(k, n, frame, start, size):
        where = spat.at[frame, :, pl.ds(pl.multiple_of(start, 128), size)]
        return remote(where, where, sp_send.at[n, k], sp_recv.at[n, k], k)

    for load in loads[1:4]:
        load.wait()
    for n, (start, size) in enumerate(CHUNKS):

        def tap(a, acc):
            lhs = xcat[pl.ds(pl.multiple_of(a * stride, 16), 2 * band * stride), :]
            rhs = convw[a, :, :, start : start + size].reshape(3 * channels, size)
            return acc + jnp.dot(lhs, rhs, preferred_element_type=jnp.float32)

        acc = lax.fori_loop(0, 3, tap, jnp.zeros((2 * band * stride, size), jnp.float32))
        acc = acc.reshape(2 * band, stride, size)[:, :width]
        column = pl.ds(pl.multiple_of(f * share + start, 128), size)
        res = latbuf[:, :, :, column].astype(jnp.float32).reshape(2 * band, width, size)
        new = res + acc + cond[:, start : start + size].reshape(1, 1, size)
        spat[r, :, column] = new.reshape(2 * cells, size).astype(jnp.bfloat16)
        for k in (3, 1, 2):
            spatial_copy(k, n, r, f * share + start, size).start()
        if n == 1:
            for k in (3, 1, 2):
                weight_arrival(k).wait_recv()
                weight_up(k, part).start()
                weight_side(k, 0, part).start()

    dec_copy.wait_recv()
    for copy in stat_copies:
        copy.wait_recv()
    dec_total = stats[0] + stats[1] + stats[2] + stats[3]
    dec_number = float(4 * cells * (dec_channels // G))
    dmean, dscale = group_norm_terms(dec_total, dec_number, dec_channels)

    def dec_act(x):
        return silu((x - dmean) * dscale * dgain_ref[...].reshape(1, -1) + dshift_ref[...].reshape(1, -1)).astype(jnp.bfloat16)

    dec_values = dec_ref[0].astype(jnp.float32).reshape(cells, dec_channels)
    middle = dec_act(dec_values)
    around = dec_act(decoth[...].astype(jnp.float32).reshape(cells, dec_channels))
    loads[4].wait()
    temporal = jnp.dot(around, timew[0], preferred_element_type=jnp.float32)
    temporal = temporal + jnp.dot(middle, timew[1], preferred_element_type=jnp.float32)
    temporal = temporal + jnp.dot(around, timew[2], preferred_element_type=jnp.float32)
    dec_out_ref[0] = (
        (dec_values + temporal).reshape(band, width, dec_channels).astype(jnp.bfloat16)
    )

    head_size = channels // HEADS
    lane = lax.broadcasted_iota(jnp.int32, (rows, 128), 0)
    low = lax.broadcasted_iota(jnp.int32, (rows, 128), 1) * head_size
    member = jnp.where((lane >= low) & (lane < low + head_size), 1.0, 0.0).astype(jnp.bfloat16)
    loads[5].wait()
    local_weight.wait()
    for k in (3, 1, 2):
        weight_up(k, part_above).wait_recv()
        weight_side(k, 1, part_above).start()
    for n, (start, size) in enumerate(CHUNKS):
        for k in (1, 2, 3):
            pf, pr = peer(k)
            spatial_copy(k, n, pr, pf * share + start, size).wait_recv()
    for k in (3, 1, 2):
        weight_side(k, 0, 2 * plane + 1 - core).wait_recv()
        weight_side(k, 1, 2 * (1 - plane) + 1 - core).wait_recv()

    def share_of(which):
        where = pl.ds(pl.multiple_of(which * cells, 16), cells)
        tokens = jnp.concatenate([spat[0, where, :], spat[1, where, :]], axis=0).astype(jnp.float32)
        mean = jnp.mean(tokens, axis=-1, keepdims=True)
        square = jnp.mean(tokens * tokens, axis=-1, keepdims=True)
        scale = lax.rsqrt(square - mean * mean + EPSILON)
        normal = ((tokens - mean) * scale * ln_ref[...].reshape(1, -1)).astype(jnp.bfloat16)
        q, k, v = [
            jnp.dot(normal, wg[i], preferred_element_type=jnp.float32)
            .astype(jnp.bfloat16)
            .astype(jnp.float32)
            for i in range(3)
        ]
        high, rest = [], []
        for a in range(2):
            for b in range(2):
                product = q[a * cells : (a + 1) * cells] * k[b * cells : (b + 1) * cells]
                top = product.astype(jnp.bfloat16)
                high.append(top)
                rest.append((product - top.astype(jnp.float32)).astype(jnp.bfloat16))
        dots = jnp.dot(
            jnp.concatenate(high + rest, axis=0), member, preferred_element_type=jnp.float32
        )
        scores = (dots[: 4 * cells] + dots[4 * cells :]) * (1.0 / math.sqrt(head_size))
        weights = jnp.exp(scores)
        probs = []
        for a in range(2):
            pair = [weights[(2 * a + b) * cells : (2 * a + b + 1) * cells] for b in range(2)]
            bottom = pair[0] + pair[1]
            probs += [(one / bottom).astype(jnp.bfloat16) for one in pair]
        spread = lax.dot_general(
            jnp.concatenate(probs, axis=0),
            member,
            (((1,), (1,)), ((), ())),
            preferred_element_type=jnp.float32,
        )
        mixed = [
            spread[2 * a * cells : (2 * a + 1) * cells] * v[:cells]
            + spread[(2 * a + 1) * cells : (2 * a + 2) * cells] * v[cells:]
            for a in range(2)
        ]
        mixed = jnp.concatenate(mixed, axis=0).astype(jnp.bfloat16)
        return jnp.dot(mixed, ow[...], preferred_element_type=jnp.float32)

    def result_copy(k):
        return remote(psend.at[k], precv.at[k], rs_send.at[k], rs_recv.at[k], k)

    def tokens_of(frame):
        return pl.ds(pl.multiple_of(frame * cells, 8), cells)

    other = share_of(1 - r).astype(jnp.bfloat16)
    far = jnp.where(f == 0, other[cells:], other[:cells])
    near = jnp.where(f == 0, other[:cells], other[cells:])
    psend[3] = far
    result_copy(3).start()
    psend[1] = near
    result_copy(1).start()
    own = share_of(r)
    psend[2] = jnp.where(f == 0, own[cells:], own[:cells]).astype(jnp.bfloat16)
    result_copy(2).start()
    mine = jnp.where(f == 0, own[:cells], own[cells:])
    where = pl.ds(pl.multiple_of(r * cells, 16), cells)
    result = spat[f, where, :].astype(jnp.float32) + mine
    for k in (3, 1, 2):
        result_copy(k).wait_recv()
        result = result + precv[k].astype(jnp.float32)
    out_ref[0] = result.reshape(band, width, channels).astype(jnp.bfloat16)

    @pl.when(f == r)
    def _():
        latent_copy(2, r).wait_send()
        for i in range(band):
            relay_forward(i, r).wait_send()

    @pl.when(f != r)
    def _():
        for i in range(band):
            relay_copy(i).wait_send()
        latent_copy(1, r).wait_send()

    dec_copy.wait_send()
    for copy in stat_copies:
        copy.wait_send()
    for k in (1, 2, 3):
        weight_copy(k).wait_send()
        weight_up(k, part).wait_send()
        weight_side(k, 0, part).wait_send()
        weight_side(k, 1, part_above).wait_send()
        result_copy(k).wait_send()
        for n, (start, size) in enumerate(CHUNKS):
            spatial_copy(k, n, r, f * share + start, size).wait_send()


def place(unet_ref, dec_ref, unet_out, dec_out, sem):
    copies = [
        pltpu.make_async_copy(unet_ref, unet_out, sem.at[0]),
        pltpu.make_async_copy(dec_ref, dec_out, sem.at[1]),
    ]
    for copy in copies:
        copy.start()
    for copy in copies:
        copy.wait()


def fused(
    latent,
    timestep,
    camera,
    dec_feat,
    norm_gain,
    norm_shift,
    emb_weight,
    conv_weight,
    ln_gain,
    q_weight,
    k_weight,
    v_weight,
    o_weight,
    dec_gain,
    dec_shift,
    time_weight,
):
    _, band, width, channels = latent.shape
    share = conv_weight.shape[3]
    rows = q_weight.shape[0]
    cells = band * width
    dec_channels = dec_feat.shape[3]
    features = conditions(timestep, camera, 2, emb_weight.shape[0] // 3)
    feats = lax.dynamic_slice_in_dim(features, lax.axis_index("row"), 1, 0)
    feats = jnp.broadcast_to(feats, (16, feats.shape[1]))
    vmem = pl.BlockSpec(memory_space=pltpu.VMEM)
    hbm = pl.BlockSpec(memory_space=pl.ANY)
    dma = pltpu.SemaphoreType.DMA
    bf16, f32 = jnp.bfloat16, jnp.float32
    unet, dec = pl.pallas_call(
        kernel,
        out_shape=(
            jax.ShapeDtypeStruct(latent.shape, bf16),
            jax.ShapeDtypeStruct(dec_feat.shape, bf16),
        ),
        in_specs=[vmem] * 8 + [hbm] * 7,
        out_specs=(vmem, vmem),
        scratch_shapes=[
            pltpu.VMEM((3, rows, channels), bf16),
            pltpu.VMEM((4, 3, rows, rows), bf16),
            pltpu.VMEM((band, width, channels), bf16),
            pltpu.VMEM(conv_weight.shape, bf16),
            pltpu.VMEM((emb_weight.shape[0], share), bf16),
            pltpu.VMEM(o_weight.shape, bf16),
            pltpu.VMEM(time_weight.shape, bf16),
            pltpu.VMEM((2, band, width, channels), bf16),
            pltpu.VMEM((6 * (width + 8), 3 * channels), bf16),
            pltpu.VMEM((2, 2 * cells, channels), bf16),
            pltpu.VMEM((3, channels, rows), bf16),
            pltpu.VMEM((band, width, dec_channels), bf16),
            pltpu.VMEM((4, 8, dec_channels), f32),
            pltpu.VMEM((4, cells, channels), bf16),
            pltpu.VMEM((4, cells, channels), bf16),
            dma((11,)),
            dma((4,)),
            dma((4,)),
            dma,
            dma,
            dma((4,)),
            dma((4,)),
            dma((4,)),
            dma((4,)),
            dma((4,)),
            dma((4,)),
            dma((2, 4)),
            dma((2, 4)),
            dma((band,)),
            dma((band,)),
            dma((3, 4)),
            dma((3, 4)),
            dma((4,)),
            dma((4,)),
        ],
        compiler_params=pltpu.CompilerParams(
            collective_id=0, has_side_effects=True, vmem_limit_bytes=60 * 1024 * 1024
        ),
        name="denoise",
    )(
        latent,
        dec_feat,
        feats,
        norm_gain,
        norm_shift,
        ln_gain,
        dec_gain,
        dec_shift,
        emb_weight,
        conv_weight,
        q_weight,
        k_weight,
        v_weight,
        o_weight,
        time_weight,
    )
    return pl.pallas_call(
        place,
        out_shape=(
            jax.ShapeDtypeStruct(latent.shape, bf16),
            jax.ShapeDtypeStruct(dec_feat.shape, bf16),
        ),
        in_specs=[vmem, vmem],
        out_specs=(hbm, hbm),
        scratch_shapes=[dma((2,))],
        name="place",
    )(unet, dec)


def solution(mesh):
    in_specs = (
        P(("asset", "frame"), "row", None, None),
        P("asset"),
        P("asset", None),
        P(("asset", "frame"), "row", None, None),
        P(),
        P(),
        P(),
        P(None, None, None, "frame"),
        P(),
        P(("frame", "row"), None),
        P(("frame", "row"), None),
        P(("frame", "row"), None),
        P(("frame", "row"), None),
        P(),
        P(),
        P(),
    )
    out_specs = (P(("asset", "frame"), "row", None, None), P(("asset", "frame"), "row", None, None))
    sizes = dict(mesh.shape)
    small = sizes["frame"] == 2 and sizes["row"] == 2 and sizes["asset"] % 4 == 0
    return jax.shard_map(fused if small else body, mesh=mesh, in_specs=in_specs, out_specs=out_specs, check_vma=False)
```

```python
import math

import jax
import jax.numpy as jnp
from jax import lax
from jax.experimental import pallas as pl
from jax.experimental.pallas import tpu as pltpu
from jax.sharding import PartitionSpec as P

HEADS = 20
G = 32


EPSILON = 1e-05


def extended(cells, sides, width):
    for axis, dim in sides:
        count = lax.axis_size(axis)
        ends = count - 1
        head = lax.slice_in_dim(cells, 0, width, axis=dim)
        tail = lax.slice_in_dim(cells, cells.shape[dim] - width, cells.shape[dim], axis=dim)
        cells = jnp.concatenate(
            [
                lax.ppermute(tail, axis, [(i, (i + 1) % count) for i in range(ends)]),
                cells,
                lax.ppermute(head, axis, [((i + 1) % count, i) for i in range(ends)]),
            ],
            axis=dim,
        )
    return cells


def from_behind(block, axis, distance):
    devices = range(lax.axis_size(axis))
    route = [((i - distance) % len(devices), i) for i in devices]
    return lax.ppermute(block, axis, route)


def sinusoids(values, entries):
    half = entries // 2
    freqs = jnp.exp(-math.log(10000.0) * jnp.arange(half, dtype=jnp.float32) / half)
    angles = values.astype(jnp.float32)[..., None] * freqs
    return jnp.concatenate([jnp.cos(angles), jnp.sin(angles)], axis=-1)


def conditions(timestep, camera, frames, entries):
    times = jnp.broadcast_to(timestep.astype(jnp.float32), (frames,))
    pieces = [
        sinusoids(times, entries),
        sinusoids(camera[:, 0], entries),
        sinusoids(camera[:, 1], entries),
    ]
    return jax.nn.silu(jnp.concatenate(pieces, axis=-1)).astype(jnp.bfloat16)


def convolve(kernel, piece):
    number, rimmed, width, channels = piece.shape
    band = rimmed - 2
    outputs = kernel.shape[3]
    widened = jnp.pad(piece, ((0, 0), (0, 0), (1, 1), (0, 0)))
    total = jnp.zeros((number * band * width, outputs), jnp.float32)
    for down in range(3):
        for side in range(3):
            window = widened[:, down : down + band, side : side + width, :].reshape(-1, channels)
            total = total + jnp.dot(window, kernel[down, side], preferred_element_type=jnp.float32)
    return total.reshape(number, band, width, outputs)


def body(
    latent,
    timestep,
    camera,
    dec_feat,
    norm_gain,
    norm_shift,
    emb_weight,
    conv_weight,
    ln_gain,
    q_weight,
    k_weight,
    v_weight,
    o_weight,
    dec_gain,
    dec_shift,
    time_weight,
):
    frame_count = lax.axis_size("frame")
    row_count = lax.axis_size("row")
    frame_index = lax.axis_index("frame")
    local_frames, band, width, channels = latent.shape
    share = conv_weight.shape[3]
    frames = local_frames * frame_count
    groups = G
    heads = HEADS
    head_size = channels // heads
    features = conditions(timestep, camera, frames, emb_weight.shape[0] // 3)
    share_start = frame_index * share
    emb_share = lax.dynamic_slice_in_dim(emb_weight, share_start, share, 1)
    cond_share = jnp.dot(features, emb_share, preferred_element_type=jnp.float32)
    values = latent.astype(jnp.float32)
    grouped = values.reshape(local_frames, band, width, groups, channels // groups)
    sums, squares = lax.psum(
        (jnp.sum(grouped, axis=(1, 2, 4)), jnp.sum(grouped * grouped, axis=(1, 2, 4))), "row"
    )
    number = band * row_count * width * (channels // groups)
    means = sums / number
    scales = lax.rsqrt(squares / number - means * means + EPSILON)
    normed = (grouped - means[:, None, None, :, None]) * scales[:, None, None, :, None]
    normed = normed.reshape(local_frames, band, width, channels) * norm_gain + norm_shift
    act = jax.nn.silu(normed).astype(jnp.bfloat16)
    residual = lax.all_to_all(latent, "frame", split_axis=3, concat_axis=0, tiled=True).astype(
        jnp.float32
    )
    rimmed = extended(act, (("row", 1),), 1)
    conv = convolve(conv_weight, lax.all_gather(rimmed, "frame", axis=0, tiled=True))
    spatial = (residual + conv + cond_share[:, None, None, :]).astype(jnp.bfloat16)
    columns = lax.all_to_all(
        spatial.reshape(frames, band * width, share),
        "frame",
        split_axis=1,
        concat_axis=2,
        tiled=True,
    )
    pixels = columns.shape[1]
    tokens = columns.astype(jnp.float32)
    token_mean = jnp.mean(tokens, axis=-1, keepdims=True)
    token_square = jnp.mean(tokens * tokens, axis=-1, keepdims=True)
    token_scale = lax.rsqrt(token_square - token_mean * token_mean + EPSILON)
    normal = (
        ((tokens - token_mean) * token_scale * ln_gain).astype(jnp.bfloat16).reshape(-1, channels)
    )
    pieces = (
        lax.all_gather(q_weight, ("frame", "row"), axis=0, tiled=True),
        lax.all_gather(k_weight, ("frame", "row"), axis=0, tiled=True),
        lax.all_gather(v_weight, ("frame", "row"), axis=0, tiled=True),
    )
    inputs = normal
    query_rows, key_rows, value_rows = tuple(
        (jnp.dot(inputs, weight_part, preferred_element_type=jnp.float32) for weight_part in pieces)
    )
    query_rows = query_rows.astype(jnp.bfloat16).reshape(frames, pixels, heads, head_size)
    key_rows = key_rows.astype(jnp.bfloat16).reshape(frames, pixels, heads, head_size)
    value_rows = value_rows.astype(jnp.bfloat16).reshape(frames, pixels, heads, head_size)
    scores = jnp.einsum(
        "fphd,gphd->phfg", query_rows, key_rows, preferred_element_type=jnp.float32
    ) * (1.0 / math.sqrt(head_size))
    weights = jnp.exp(scores)
    probs = (weights / jnp.sum(weights, axis=-1, keepdims=True)).astype(jnp.bfloat16)
    mixed = (
        jnp.einsum("phfg,gphd->fphd", probs, value_rows, preferred_element_type=jnp.float32)
        .astype(jnp.bfloat16)
        .reshape(-1, channels)
    )
    inputs = mixed
    attended = jnp.dot(
        inputs,
        lax.all_gather(o_weight, ("frame", "row"), axis=0, tiled=True),
        preferred_element_type=jnp.float32,
    )
    result = (
        (tokens.reshape(-1, channels) + attended)
        .astype(jnp.bfloat16)
        .reshape(frames, pixels, channels)
    )
    unet_out = lax.all_to_all(result, "frame", split_axis=0, concat_axis=1, tiled=True).reshape(
        local_frames, band, width, channels
    )
    dec_frames, dec_band, dec_width, dec_channels = dec_feat.shape
    dec_values = dec_feat.astype(jnp.float32)
    dec_grouped = dec_values.reshape(
        dec_frames, dec_band, dec_width, groups, dec_channels // groups
    )
    dec_sums, dec_squares = lax.psum(
        (
            jnp.sum(dec_grouped, axis=(0, 1, 2, 4)),
            jnp.sum(dec_grouped * dec_grouped, axis=(0, 1, 2, 4)),
        ),
        ("frame", "row"),
    )
    dec_number = (
        dec_frames * frame_count * dec_band * row_count * dec_width * (dec_channels // groups)
    )
    dec_means = dec_sums / dec_number
    dec_scales = lax.rsqrt(dec_squares / dec_number - dec_means * dec_means + EPSILON)
    dec_normed = ((dec_grouped - dec_means[:, None]) * dec_scales[:, None]).reshape(
        dec_frames, dec_band, dec_width, dec_channels
    )
    dec_act = jax.nn.silu(dec_normed * dec_gain + dec_shift).astype(jnp.bfloat16)
    earlier = from_behind(dec_act, "frame", 1)
    later = from_behind(dec_act, "frame", -1)
    before = jnp.concatenate([earlier, dec_act[:-1]], axis=0).reshape(-1, dec_channels)
    after = jnp.concatenate([dec_act[1:], later], axis=0).reshape(-1, dec_channels)
    middle = dec_act.reshape(-1, dec_channels)
    temporal = jnp.dot(before, time_weight[0], preferred_element_type=jnp.float32)
    temporal = temporal + jnp.dot(middle, time_weight[1], preferred_element_type=jnp.float32)
    temporal = temporal + jnp.dot(after, time_weight[2], preferred_element_type=jnp.float32)
    dec_out = (dec_values + temporal.reshape(dec_frames, dec_band, dec_width, dec_channels)).astype(
        jnp.bfloat16
    )
    return (unet_out, dec_out)


def silu(x):
    return x * jax.nn.sigmoid(x)


def group_matrix(channels, groups):
    size = channels // groups
    channel = lax.broadcasted_iota(jnp.int32, (channels, 128), 0)
    low = lax.broadcasted_iota(jnp.int32, (channels, 128), 1) * size
    return jnp.where((channel >= low) & (channel < low + size), 1.0, 0.0).astype(jnp.float32)


def group_norm_terms(sums, number, channels):
    member = group_matrix(channels, G)
    grouped = jnp.dot(
        sums, member, precision=lax.Precision.HIGHEST, preferred_element_type=jnp.float32
    )
    spread = lax.dot_general(
        grouped,
        member,
        (((1,), (1,)), ((), ())),
        precision=lax.Precision.HIGHEST,
        preferred_element_type=jnp.float32,
    )
    mean = spread[0:1] / number
    square = spread[1:2] / number
    return mean, lax.rsqrt(square - mean * mean + EPSILON)


CHUNKS = ((0, 256), (256, 256), (512, 128))


def kernel(
    latent_ref,
    dec_ref,
    feats_ref,
    gain_ref,
    shift_ref,
    ln_ref,
    dgain_ref,
    dshift_ref,
    emb_hbm,
    conv_hbm,
    q_hbm,
    k_hbm,
    v_hbm,
    o_hbm,
    time_hbm,
    out_ref,
    dec_out_ref,
    wraw,
    wsend,
    relay,
    convw,
    emb,
    ow,
    timew,
    latbuf,
    xcat,
    spat,
    wg,
    decoth,
    stats,
    psend,
    precv,
    load_sem,
    lat_send,
    lat_recv,
    dec_send,
    dec_recv,
    st_send,
    st_recv,
    w_send,
    w_recv,
    zw_send,
    zw_recv,
    fw_send,
    fw_recv,
    rl_send,
    rl_recv,
    sp_send,
    sp_recv,
    rs_send,
    rs_recv,
):
    MESH = pl.DeviceIdType.MESH
    asset = lax.axis_index("asset")
    f = lax.axis_index("frame")
    r = lax.axis_index("row")
    core = asset % 2
    plane = asset // 2 % 2
    sibling = asset + 1 - 2 * core
    above = asset + 2 - 4 * plane
    me = 2 * f + r
    _, band, width, channels = latent_ref.shape
    cells = band * width
    share = convw.shape[3]
    rows = ow.shape[0]
    quarter = rows // 4
    part = 2 * plane + core
    part_above = 2 * (1 - plane) + core
    dec_channels = dec_ref.shape[3]
    stride = width + 8

    def peer(k):
        pf = 1 - f if k >= 2 else f
        pr = 1 - r if k % 2 else r
        return pf, pr

    def remote(src, dst, send, recv, k):
        pf, pr = peer(k)
        return pltpu.make_async_remote_copy(
            src_ref=src,
            dst_ref=dst,
            send_sem=send,
            recv_sem=recv,
            device_id=(asset, pf, pr),
            device_id_type=MESH,
        )

    raw = [
        pltpu.make_async_copy(ref, wraw.at[i], load_sem.at[8 + i])
        for i, ref in enumerate((q_hbm, k_hbm, v_hbm))
    ]
    for load in raw:
        load.start()
    loads = [
        pltpu.make_async_copy(
            emb_hbm.at[:, pl.ds(pl.multiple_of(f * share, 128), share)], emb, load_sem.at[0]
        ),
        pltpu.make_async_copy(conv_hbm.at[0], convw.at[0], load_sem.at[1]),
        pltpu.make_async_copy(conv_hbm.at[1], convw.at[1], load_sem.at[2]),
        pltpu.make_async_copy(conv_hbm.at[2], convw.at[2], load_sem.at[3]),
        pltpu.make_async_copy(time_hbm, timew, load_sem.at[4]),
        pltpu.make_async_copy(o_hbm, ow, load_sem.at[5]),
    ]
    for load in loads:
        load.start()

    barrier = pltpu.get_barrier_semaphore()
    for k in (1, 2, 3):
        pf, pr = peer(k)
        pl.semaphore_signal(barrier, inc=1, device_id=(asset, pf, pr), device_id_type=MESH)
    for other_asset in (sibling, above):
        pl.semaphore_signal(barrier, inc=1, device_id=(other_asset, f, r), device_id_type=MESH)
    pl.semaphore_wait(barrier, 5)

    def latent_copy(k, slot):
        return remote(latent_ref.at[0], latbuf.at[slot], lat_send.at[k], lat_recv.at[k], k)

    local_latent = pltpu.make_async_copy(latent_ref.at[0], latbuf.at[r], load_sem.at[7])

    def relay_copy(i):
        return remote(latent_ref.at[0, i], relay.at[i], rl_send.at[i], rl_recv.at[i], 2)

    def relay_forward(i, slot):
        return remote(relay.at[i], latbuf.at[slot, i], rl_send.at[i], rl_recv.at[i], 1)

    @pl.when(f == r)
    def _():
        latent_copy(2, r).start()
        local_latent.start()

    @pl.when(f != r)
    def _():
        for i in range(band):
            relay_copy(i).start()
        latent_copy(1, r).start()

    dec_copy = remote(dec_ref.at[0], decoth, dec_send, dec_recv, 2)
    dec_copy.start()

    dec_own = dec_ref[0].astype(jnp.float32).reshape(cells, dec_channels)
    dec_sum = jnp.sum(dec_own, axis=0, keepdims=True)
    dec_square = jnp.sum(dec_own * dec_own, axis=0, keepdims=True)
    stats[0] = jnp.concatenate(
        [dec_sum, dec_square, jnp.zeros((6, dec_channels), jnp.float32)], axis=0
    )
    stat_copies = [
        remote(stats.at[0], stats.at[k], st_send.at[k], st_recv.at[k], k) for k in (1, 2, 3)
    ]
    for copy in stat_copies:
        copy.start()

    for load in raw:
        load.wait()
    for i in range(3):
        for target in range(4):
            wsend[target, i] = wraw[i, :, target * rows : (target + 1) * rows]
    local_weight = pltpu.make_async_copy(
        wsend.at[me], wg.at[:, pl.ds(pl.multiple_of(me * rows, 16), rows), :], load_sem.at[6]
    )
    local_weight.start()

    loads[0].wait()
    cond = jnp.dot(feats_ref[...], emb[...], preferred_element_type=jnp.float32)[0:1]

    xcat[0:stride, :] = jnp.zeros((stride, 3 * channels), jnp.bfloat16)
    xcat[5 * stride : 6 * stride, :] = jnp.zeros((stride, 3 * channels), jnp.bfloat16)

    @pl.when(f == r)
    def _():
        local_latent.wait()
        for i in range(band):
            relay_copy(i).wait_recv()
            relay_forward(i, r).start()
        latent_copy(1, 1 - r).wait_recv()

    @pl.when(f != r)
    def _():
        latent_copy(2, r).wait_recv()
        for i in range(band):
            relay_forward(i, 1 - r).wait_recv()

    def source_rows(k, which):
        pf, pr = peer(k)
        source = 2 * pf + pr
        return pl.ds(pl.multiple_of(source * rows + which * quarter, 16), quarter)

    def weight_copy(k):
        pf, pr = peer(k)
        target = 2 * pf + pr
        mine = pl.ds(pl.multiple_of(part * quarter, 16), quarter)
        there = pl.ds(pl.multiple_of(me * rows + part * quarter, 16), quarter)
        return remote(
            wsend.at[target, :, mine, :], wg.at[:, there, :], w_send.at[k], w_recv.at[k], k
        )

    def weight_arrival(k):
        where = wg.at[:, source_rows(k, part), :]
        return remote(where, where, w_send.at[k], w_recv.at[k], k)

    def weight_pass(k, which, send, recv, other_asset):
        where = wg.at[:, source_rows(k, which), :]
        return pltpu.make_async_remote_copy(
            src_ref=where,
            dst_ref=where,
            send_sem=send,
            recv_sem=recv,
            device_id=(other_asset, f, r),
            device_id_type=MESH,
        )

    def weight_up(k, which):
        return weight_pass(k, which, zw_send.at[k], zw_recv.at[k], above)

    def weight_side(k, j, which):
        return weight_pass(k, which, fw_send.at[j, k], fw_recv.at[j, k], sibling)

    for k in (3, 1, 2):
        weight_copy(k).start()

    total = jnp.zeros((1, channels), jnp.float32)
    square = jnp.zeros((1, channels), jnp.float32)
    for i in range(2 * band):
        x = latbuf[i // band, i % band].astype(jnp.float32)
        total = total + jnp.sum(x, axis=0, keepdims=True)
        square = square + jnp.sum(x * x, axis=0, keepdims=True)
    sums = jnp.concatenate([total, square, jnp.zeros((6, channels), jnp.float32)], axis=0)
    number = float(2 * cells * (channels // G))
    mean, scale = group_norm_terms(sums, number, channels)
    for i in range(2 * band):
        x = latbuf[i // band, i % band].astype(jnp.float32)
        act = silu((x - mean) * scale * gain_ref[...].reshape(1, -1) + shift_ref[...].reshape(1, -1))
        padded = jnp.concatenate([act, jnp.zeros((8, channels), jnp.float32)], axis=0)
        at = slice((i + 1) * stride, (i + 2) * stride)
        xcat[at, 0:channels] = pltpu.roll(padded, 1, 0).astype(jnp.bfloat16)
        xcat[at, channels : 2 * channels] = padded.astype(jnp.bfloat16)
        xcat[at, 2 * channels :] = pltpu.roll(padded, stride - 1, 0).astype(jnp.bfloat16)

    def spatial_copy(k, n, frame, start, size):
        where = spat.at[frame, :, pl.ds(pl.multiple_of(start, 128), size)]
        return remote(where, where, sp_send.at[n, k], sp_recv.at[n, k], k)

    def entry(n):
        return 1 if n == 1 else 2

    def pass_on(n):
        start, size = CHUNKS[n]
        pf, pr = peer(entry(n))
        spatial_copy(entry(n), n, pr, pf * share + start, size).wait_recv()
        where = spat.at[pr, :, pl.ds(pl.multiple_of(pf * share + start, 128), size)]
        remote(where, where, sp_send.at[n, 3], sp_recv.at[n, 3], 3 - entry(n)).start()

    for load in loads[1:4]:
        load.wait()
    for n, (start, size) in enumerate(CHUNKS):

        def tap(a, acc):
            lhs = xcat[pl.ds(pl.multiple_of(a * stride, 16), 2 * band * stride), :]
            rhs = convw[a, :, :, start : start + size].reshape(3 * channels, size)
            return acc + jnp.dot(lhs, rhs, preferred_element_type=jnp.float32)

        acc = lax.fori_loop(0, 3, tap, jnp.zeros((2 * band * stride, size), jnp.float32))
        acc = acc.reshape(2 * band, stride, size)[:, :width]
        column = pl.ds(pl.multiple_of(f * share + start, 128), size)
        res = latbuf[:, :, :, column].astype(jnp.float32).reshape(2 * band, width, size)
        new = res + acc + cond[:, start : start + size].reshape(1, 1, size)
        spat[r, :, column] = new.reshape(2 * cells, size).astype(jnp.bfloat16)
        for k in (1, 2):
            spatial_copy(k, n, r, f * share + start, size).start()
        if n == 1:
            for k in (3, 1, 2):
                weight_arrival(k).wait_recv()
                weight_up(k, part).start()
                weight_side(k, 0, part).start()

    pass_on(0)
    pass_on(1)

    dec_copy.wait_recv()
    for copy in stat_copies:
        copy.wait_recv()
    dec_total = stats[0] + stats[1] + stats[2] + stats[3]
    dec_number = float(4 * cells * (dec_channels // G))
    dmean, dscale = group_norm_terms(dec_total, dec_number, dec_channels)

    def dec_act(x):
        return silu((x - dmean) * dscale * dgain_ref[...].reshape(1, -1) + dshift_ref[...].reshape(1, -1)).astype(jnp.bfloat16)

    dec_values = dec_ref[0].astype(jnp.float32).reshape(cells, dec_channels)
    middle = dec_act(dec_values)
    around = dec_act(decoth[...].astype(jnp.float32).reshape(cells, dec_channels))
    loads[4].wait()
    temporal = jnp.dot(around, timew[0], preferred_element_type=jnp.float32)
    temporal = temporal + jnp.dot(middle, timew[1], preferred_element_type=jnp.float32)
    temporal = temporal + jnp.dot(around, timew[2], preferred_element_type=jnp.float32)
    dec_out_ref[0] = (
        (dec_values + temporal).reshape(band, width, dec_channels).astype(jnp.bfloat16)
    )

    pass_on(2)

    head_size = channels // HEADS
    lane = lax.broadcasted_iota(jnp.int32, (rows, 128), 0)
    low = lax.broadcasted_iota(jnp.int32, (rows, 128), 1) * head_size
    member = jnp.where((lane >= low) & (lane < low + head_size), 1.0, 0.0).astype(jnp.bfloat16)
    loads[5].wait()
    local_weight.wait()
    for k in (3, 1, 2):
        weight_up(k, part_above).wait_recv()
        weight_side(k, 1, part_above).start()
    for n, (start, size) in enumerate(CHUNKS):
        for k in (3 - entry(n), 3):
            pf, pr = peer(k)
            spatial_copy(k, n, pr, pf * share + start, size).wait_recv()
    for k in (3, 1, 2):
        weight_side(k, 0, 2 * plane + 1 - core).wait_recv()
        weight_side(k, 1, 2 * (1 - plane) + 1 - core).wait_recv()

    def share_of(which):
        where = pl.ds(pl.multiple_of(which * cells, 16), cells)
        tokens = jnp.concatenate([spat[0, where, :], spat[1, where, :]], axis=0).astype(jnp.float32)
        mean = jnp.mean(tokens, axis=-1, keepdims=True)
        square = jnp.mean(tokens * tokens, axis=-1, keepdims=True)
        scale = lax.rsqrt(square - mean * mean + EPSILON)
        normal = ((tokens - mean) * scale * ln_ref[...].reshape(1, -1)).astype(jnp.bfloat16)
        q, k, v = [
            jnp.dot(normal, wg[i], preferred_element_type=jnp.float32)
            .astype(jnp.bfloat16)
            .astype(jnp.float32)
            for i in range(3)
        ]
        high, rest = [], []
        for a in range(2):
            for b in range(2):
                product = q[a * cells : (a + 1) * cells] * k[b * cells : (b + 1) * cells]
                top = product.astype(jnp.bfloat16)
                high.append(top)
                rest.append((product - top.astype(jnp.float32)).astype(jnp.bfloat16))
        dots = jnp.dot(
            jnp.concatenate(high + rest, axis=0), member, preferred_element_type=jnp.float32
        )
        scores = (dots[: 4 * cells] + dots[4 * cells :]) * (1.0 / math.sqrt(head_size))
        weights = jnp.exp(scores)
        probs = []
        for a in range(2):
            pair = [weights[(2 * a + b) * cells : (2 * a + b + 1) * cells] for b in range(2)]
            bottom = pair[0] + pair[1]
            probs += [(one / bottom).astype(jnp.bfloat16) for one in pair]
        spread = lax.dot_general(
            jnp.concatenate(probs, axis=0),
            member,
            (((1,), (1,)), ((), ())),
            preferred_element_type=jnp.float32,
        )
        mixed = [
            spread[2 * a * cells : (2 * a + 1) * cells] * v[:cells]
            + spread[(2 * a + 1) * cells : (2 * a + 2) * cells] * v[cells:]
            for a in range(2)
        ]
        mixed = jnp.concatenate(mixed, axis=0).astype(jnp.bfloat16)
        return jnp.dot(mixed, ow[...], preferred_element_type=jnp.float32)

    middle_channel = channels // 2
    left = slice(0, middle_channel)
    right = slice(middle_channel, channels)

    def result_copy(i):
        slot, k, side = ((3, 1, 0), (3, 2, 1), (1, 1, 0), (1, 1, 1), (2, 2, 0), (2, 2, 1))[i]
        columns = pl.ds(side * middle_channel, middle_channel)
        return remote(
            psend.at[slot, :, columns], precv.at[slot, :, columns], rs_send.at[i], rs_recv.at[i], k
        )

    other = share_of(1 - r)
    far = jnp.where(f == 0, other[cells:], other[:cells])
    near = jnp.where(f == 0, other[:cells], other[cells:])
    psend[3] = far.astype(jnp.bfloat16)
    result_copy(1).start()
    result_copy(0).start()
    psend[1, :, left] = near[:, left].astype(jnp.bfloat16)
    result_copy(2).start()
    own = share_of(r)
    second = jnp.where(f == 0, own[cells:], own[:cells])
    mine = jnp.where(f == 0, own[:cells], own[cells:])
    psend[2, :, right] = second[:, right].astype(jnp.bfloat16)
    result_copy(5).start()
    result_copy(0).wait_recv()
    psend[2, :, left] = (second[:, left] + precv[3, :, left].astype(jnp.float32)).astype(
        jnp.bfloat16
    )
    result_copy(4).start()
    result_copy(1).wait_recv()
    psend[1, :, right] = (near[:, right] + precv[3, :, right].astype(jnp.float32)).astype(
        jnp.bfloat16
    )
    result_copy(3).start()
    where = pl.ds(pl.multiple_of(r * cells, 16), cells)
    result = spat[f, where, :].astype(jnp.float32) + mine
    for i in (2, 3, 4, 5):
        result_copy(i).wait_recv()
    result = result + precv[1].astype(jnp.float32) + precv[2].astype(jnp.float32)
    out_ref[0] = result.reshape(band, width, channels).astype(jnp.bfloat16)

    @pl.when(f == r)
    def _():
        latent_copy(2, r).wait_send()
        for i in range(band):
            relay_forward(i, r).wait_send()

    @pl.when(f != r)
    def _():
        for i in range(band):
            relay_copy(i).wait_send()
        latent_copy(1, r).wait_send()

    dec_copy.wait_send()
    for copy in stat_copies:
        copy.wait_send()
    for i in range(6):
        result_copy(i).wait_send()
    for k in (1, 2, 3):
        weight_copy(k).wait_send()
        weight_up(k, part).wait_send()
        weight_side(k, 0, part).wait_send()
        weight_side(k, 1, part_above).wait_send()
        for n, (start, size) in enumerate(CHUNKS):
            spatial_copy(k, n, r, f * share + start, size).wait_send()


def place(unet_ref, dec_ref, unet_out, dec_out, sem):
    copies = [
        pltpu.make_async_copy(unet_ref, unet_out, sem.at[0]),
        pltpu.make_async_copy(dec_ref, dec_out, sem.at[1]),
    ]
    for copy in copies:
        copy.start()
    for copy in copies:
        copy.wait()


def fused(
    latent,
    timestep,
    camera,
    dec_feat,
    norm_gain,
    norm_shift,
    emb_weight,
    conv_weight,
    ln_gain,
    q_weight,
    k_weight,
    v_weight,
    o_weight,
    dec_gain,
    dec_shift,
    time_weight,
):
    _, band, width, channels = latent.shape
    share = conv_weight.shape[3]
    rows = q_weight.shape[0]
    cells = band * width
    dec_channels = dec_feat.shape[3]
    features = conditions(timestep, camera, 2, emb_weight.shape[0] // 3)
    feats = lax.dynamic_slice_in_dim(features, lax.axis_index("row"), 1, 0)
    feats = jnp.broadcast_to(feats, (16, feats.shape[1]))
    vmem = pl.BlockSpec(memory_space=pltpu.VMEM)
    hbm = pl.BlockSpec(memory_space=pl.ANY)
    dma = pltpu.SemaphoreType.DMA
    bf16, f32 = jnp.bfloat16, jnp.float32
    unet, dec = pl.pallas_call(
        kernel,
        out_shape=(
            jax.ShapeDtypeStruct(latent.shape, bf16),
            jax.ShapeDtypeStruct(dec_feat.shape, bf16),
        ),
        in_specs=[vmem] * 8 + [hbm] * 7,
        out_specs=(vmem, vmem),
        scratch_shapes=[
            pltpu.VMEM((3, rows, channels), bf16),
            pltpu.VMEM((4, 3, rows, rows), bf16),
            pltpu.VMEM((band, width, channels), bf16),
            pltpu.VMEM(conv_weight.shape, bf16),
            pltpu.VMEM((emb_weight.shape[0], share), bf16),
            pltpu.VMEM(o_weight.shape, bf16),
            pltpu.VMEM(time_weight.shape, bf16),
            pltpu.VMEM((2, band, width, channels), bf16),
            pltpu.VMEM((6 * (width + 8), 3 * channels), bf16),
            pltpu.VMEM((2, 2 * cells, channels), bf16),
            pltpu.VMEM((3, channels, rows), bf16),
            pltpu.VMEM((band, width, dec_channels), bf16),
            pltpu.VMEM((4, 8, dec_channels), f32),
            pltpu.VMEM((4, cells, channels), bf16),
            pltpu.VMEM((4, cells, channels), bf16),
            dma((11,)),
            dma((4,)),
            dma((4,)),
            dma,
            dma,
            dma((4,)),
            dma((4,)),
            dma((4,)),
            dma((4,)),
            dma((4,)),
            dma((4,)),
            dma((2, 4)),
            dma((2, 4)),
            dma((band,)),
            dma((band,)),
            dma((3, 4)),
            dma((3, 4)),
            dma((6,)),
            dma((6,)),
        ],
        compiler_params=pltpu.CompilerParams(
            collective_id=0, has_side_effects=True, vmem_limit_bytes=60 * 1024 * 1024
        ),
        name="denoise",
    )(
        latent,
        dec_feat,
        feats,
        norm_gain,
        norm_shift,
        ln_gain,
        dec_gain,
        dec_shift,
        emb_weight,
        conv_weight,
        q_weight,
        k_weight,
        v_weight,
        o_weight,
        time_weight,
    )
    return pl.pallas_call(
        place,
        out_shape=(
            jax.ShapeDtypeStruct(latent.shape, bf16),
            jax.ShapeDtypeStruct(dec_feat.shape, bf16),
        ),
        in_specs=[vmem, vmem],
        out_specs=(hbm, hbm),
        scratch_shapes=[dma((2,))],
        name="place",
    )(unet, dec)


def solution(mesh):
    in_specs = (
        P(("asset", "frame"), "row", None, None),
        P("asset"),
        P("asset", None),
        P(("asset", "frame"), "row", None, None),
        P(),
        P(),
        P(),
        P(None, None, None, "frame"),
        P(),
        P(("frame", "row"), None),
        P(("frame", "row"), None),
        P(("frame", "row"), None),
        P(("frame", "row"), None),
        P(),
        P(),
        P(),
    )
    out_specs = (P(("asset", "frame"), "row", None, None), P(("asset", "frame"), "row", None, None))
    sizes = dict(mesh.shape)
    small = sizes["frame"] == 2 and sizes["row"] == 2 and sizes["asset"] % 4 == 0
    return jax.shard_map(fused if small else body, mesh=mesh, in_specs=in_specs, out_specs=out_specs, check_vma=False)
```

```python
import math

import jax
import jax.numpy as jnp
from jax import lax
from jax.experimental import pallas as pl
from jax.experimental.pallas import tpu as pltpu
from jax.sharding import PartitionSpec as P

HEADS = 20
G = 32


EPSILON = 1e-05


def extended(cells, sides, width):
    for axis, dim in sides:
        count = lax.axis_size(axis)
        ends = count - 1
        head = lax.slice_in_dim(cells, 0, width, axis=dim)
        tail = lax.slice_in_dim(cells, cells.shape[dim] - width, cells.shape[dim], axis=dim)
        cells = jnp.concatenate(
            [
                lax.ppermute(tail, axis, [(i, (i + 1) % count) for i in range(ends)]),
                cells,
                lax.ppermute(head, axis, [((i + 1) % count, i) for i in range(ends)]),
            ],
            axis=dim,
        )
    return cells


def from_behind(block, axis, distance):
    devices = range(lax.axis_size(axis))
    route = [((i - distance) % len(devices), i) for i in devices]
    return lax.ppermute(block, axis, route)


def sinusoids(values, entries):
    half = entries // 2
    freqs = jnp.exp(-math.log(10000.0) * jnp.arange(half, dtype=jnp.float32) / half)
    angles = values.astype(jnp.float32)[..., None] * freqs
    return jnp.concatenate([jnp.cos(angles), jnp.sin(angles)], axis=-1)


def conditions(timestep, camera, frames, entries):
    times = jnp.broadcast_to(timestep.astype(jnp.float32), (frames,))
    pieces = [
        sinusoids(times, entries),
        sinusoids(camera[:, 0], entries),
        sinusoids(camera[:, 1], entries),
    ]
    return jax.nn.silu(jnp.concatenate(pieces, axis=-1)).astype(jnp.bfloat16)


def convolve(kernel, piece):
    number, rimmed, width, channels = piece.shape
    band = rimmed - 2
    outputs = kernel.shape[3]
    widened = jnp.pad(piece, ((0, 0), (0, 0), (1, 1), (0, 0)))
    total = jnp.zeros((number * band * width, outputs), jnp.float32)
    for down in range(3):
        for side in range(3):
            window = widened[:, down : down + band, side : side + width, :].reshape(-1, channels)
            total = total + jnp.dot(window, kernel[down, side], preferred_element_type=jnp.float32)
    return total.reshape(number, band, width, outputs)


def body(
    latent,
    timestep,
    camera,
    dec_feat,
    norm_gain,
    norm_shift,
    emb_weight,
    conv_weight,
    ln_gain,
    q_weight,
    k_weight,
    v_weight,
    o_weight,
    dec_gain,
    dec_shift,
    time_weight,
):
    frame_count = lax.axis_size("frame")
    row_count = lax.axis_size("row")
    frame_index = lax.axis_index("frame")
    local_frames, band, width, channels = latent.shape
    share = conv_weight.shape[3]
    frames = local_frames * frame_count
    groups = G
    heads = HEADS
    head_size = channels // heads
    features = conditions(timestep, camera, frames, emb_weight.shape[0] // 3)
    share_start = frame_index * share
    emb_share = lax.dynamic_slice_in_dim(emb_weight, share_start, share, 1)
    cond_share = jnp.dot(features, emb_share, preferred_element_type=jnp.float32)
    values = latent.astype(jnp.float32)
    grouped = values.reshape(local_frames, band, width, groups, channels // groups)
    sums, squares = lax.psum(
        (jnp.sum(grouped, axis=(1, 2, 4)), jnp.sum(grouped * grouped, axis=(1, 2, 4))), "row"
    )
    number = band * row_count * width * (channels // groups)
    means = sums / number
    scales = lax.rsqrt(squares / number - means * means + EPSILON)
    normed = (grouped - means[:, None, None, :, None]) * scales[:, None, None, :, None]
    normed = normed.reshape(local_frames, band, width, channels) * norm_gain + norm_shift
    act = jax.nn.silu(normed).astype(jnp.bfloat16)
    residual = lax.all_to_all(latent, "frame", split_axis=3, concat_axis=0, tiled=True).astype(
        jnp.float32
    )
    rimmed = extended(act, (("row", 1),), 1)
    conv = convolve(conv_weight, lax.all_gather(rimmed, "frame", axis=0, tiled=True))
    spatial = (residual + conv + cond_share[:, None, None, :]).astype(jnp.bfloat16)
    columns = lax.all_to_all(
        spatial.reshape(frames, band * width, share),
        "frame",
        split_axis=1,
        concat_axis=2,
        tiled=True,
    )
    pixels = columns.shape[1]
    tokens = columns.astype(jnp.float32)
    token_mean = jnp.mean(tokens, axis=-1, keepdims=True)
    token_square = jnp.mean(tokens * tokens, axis=-1, keepdims=True)
    token_scale = lax.rsqrt(token_square - token_mean * token_mean + EPSILON)
    normal = (
        ((tokens - token_mean) * token_scale * ln_gain).astype(jnp.bfloat16).reshape(-1, channels)
    )
    pieces = (
        lax.all_gather(q_weight, ("frame", "row"), axis=0, tiled=True),
        lax.all_gather(k_weight, ("frame", "row"), axis=0, tiled=True),
        lax.all_gather(v_weight, ("frame", "row"), axis=0, tiled=True),
    )
    inputs = normal
    query_rows, key_rows, value_rows = tuple(
        (jnp.dot(inputs, weight_part, preferred_element_type=jnp.float32) for weight_part in pieces)
    )
    query_rows = query_rows.astype(jnp.bfloat16).reshape(frames, pixels, heads, head_size)
    key_rows = key_rows.astype(jnp.bfloat16).reshape(frames, pixels, heads, head_size)
    value_rows = value_rows.astype(jnp.bfloat16).reshape(frames, pixels, heads, head_size)
    scores = jnp.einsum(
        "fphd,gphd->phfg", query_rows, key_rows, preferred_element_type=jnp.float32
    ) * (1.0 / math.sqrt(head_size))
    weights = jnp.exp(scores)
    probs = (weights / jnp.sum(weights, axis=-1, keepdims=True)).astype(jnp.bfloat16)
    mixed = (
        jnp.einsum("phfg,gphd->fphd", probs, value_rows, preferred_element_type=jnp.float32)
        .astype(jnp.bfloat16)
        .reshape(-1, channels)
    )
    inputs = mixed
    attended = jnp.dot(
        inputs,
        lax.all_gather(o_weight, ("frame", "row"), axis=0, tiled=True),
        preferred_element_type=jnp.float32,
    )
    result = (
        (tokens.reshape(-1, channels) + attended)
        .astype(jnp.bfloat16)
        .reshape(frames, pixels, channels)
    )
    unet_out = lax.all_to_all(result, "frame", split_axis=0, concat_axis=1, tiled=True).reshape(
        local_frames, band, width, channels
    )
    dec_frames, dec_band, dec_width, dec_channels = dec_feat.shape
    dec_values = dec_feat.astype(jnp.float32)
    dec_grouped = dec_values.reshape(
        dec_frames, dec_band, dec_width, groups, dec_channels // groups
    )
    dec_sums, dec_squares = lax.psum(
        (
            jnp.sum(dec_grouped, axis=(0, 1, 2, 4)),
            jnp.sum(dec_grouped * dec_grouped, axis=(0, 1, 2, 4)),
        ),
        ("frame", "row"),
    )
    dec_number = (
        dec_frames * frame_count * dec_band * row_count * dec_width * (dec_channels // groups)
    )
    dec_means = dec_sums / dec_number
    dec_scales = lax.rsqrt(dec_squares / dec_number - dec_means * dec_means + EPSILON)
    dec_normed = ((dec_grouped - dec_means[:, None]) * dec_scales[:, None]).reshape(
        dec_frames, dec_band, dec_width, dec_channels
    )
    dec_act = jax.nn.silu(dec_normed * dec_gain + dec_shift).astype(jnp.bfloat16)
    earlier = from_behind(dec_act, "frame", 1)
    later = from_behind(dec_act, "frame", -1)
    before = jnp.concatenate([earlier, dec_act[:-1]], axis=0).reshape(-1, dec_channels)
    after = jnp.concatenate([dec_act[1:], later], axis=0).reshape(-1, dec_channels)
    middle = dec_act.reshape(-1, dec_channels)
    temporal = jnp.dot(before, time_weight[0], preferred_element_type=jnp.float32)
    temporal = temporal + jnp.dot(middle, time_weight[1], preferred_element_type=jnp.float32)
    temporal = temporal + jnp.dot(after, time_weight[2], preferred_element_type=jnp.float32)
    dec_out = (dec_values + temporal.reshape(dec_frames, dec_band, dec_width, dec_channels)).astype(
        jnp.bfloat16
    )
    return (unet_out, dec_out)


def silu(x):
    return x * jax.nn.sigmoid(x)


def group_matrix(channels, groups):
    size = channels // groups
    channel = lax.broadcasted_iota(jnp.int32, (channels, 128), 0)
    low = lax.broadcasted_iota(jnp.int32, (channels, 128), 1) * size
    return jnp.where((channel >= low) & (channel < low + size), 1.0, 0.0).astype(jnp.float32)


def group_norm_terms(sums, number, channels):
    member = group_matrix(channels, G)
    grouped = jnp.dot(
        sums, member, precision=lax.Precision.HIGHEST, preferred_element_type=jnp.float32
    )
    spread = lax.dot_general(
        grouped,
        member,
        (((1,), (1,)), ((), ())),
        precision=lax.Precision.HIGHEST,
        preferred_element_type=jnp.float32,
    )
    mean = spread[0:1] / number
    square = spread[1:2] / number
    return mean, lax.rsqrt(square - mean * mean + EPSILON)


CHUNKS = ((0, 256), (256, 256), (512, 128))


def kernel(
    latent_ref,
    dec_ref,
    time_ref,
    camera_ref,
    gain_ref,
    shift_ref,
    ln_ref,
    dgain_ref,
    dshift_ref,
    emb_hbm,
    conv_hbm,
    q_hbm,
    k_hbm,
    v_hbm,
    o_hbm,
    time_hbm,
    out_ref,
    dec_out_ref,
    wraw,
    wsend,
    relay,
    convw,
    emb,
    ow,
    timew,
    latbuf,
    xcat,
    spat,
    wg,
    decoth,
    stats,
    psend,
    precv,
    load_sem,
    lat_send,
    lat_recv,
    dec_send,
    dec_recv,
    st_send,
    st_recv,
    w_send,
    w_recv,
    zw_send,
    zw_recv,
    fw_send,
    fw_recv,
    rl_send,
    rl_recv,
    sp_send,
    sp_recv,
    rs_send,
    rs_recv,
):
    MESH = pl.DeviceIdType.MESH
    asset = lax.axis_index("asset")
    f = lax.axis_index("frame")
    r = lax.axis_index("row")
    core = asset % 2
    plane = asset // 2 % 2
    sibling = asset + 1 - 2 * core
    above = asset + 2 - 4 * plane
    me = 2 * f + r
    _, band, width, channels = latent_ref.shape
    cells = band * width
    share = convw.shape[3]
    rows = ow.shape[0]
    quarter = rows // 4
    part = 2 * plane + core
    part_above = 2 * (1 - plane) + core
    dec_channels = dec_ref.shape[3]
    stride = width + 8

    def peer(k):
        pf = 1 - f if k >= 2 else f
        pr = 1 - r if k % 2 else r
        return pf, pr

    def remote(src, dst, send, recv, k):
        pf, pr = peer(k)
        return pltpu.make_async_remote_copy(
            src_ref=src,
            dst_ref=dst,
            send_sem=send,
            recv_sem=recv,
            device_id=(asset, pf, pr),
            device_id_type=MESH,
        )

    raw = [
        pltpu.make_async_copy(ref, wraw.at[i], load_sem.at[8 + i])
        for i, ref in enumerate((q_hbm, k_hbm, v_hbm))
    ]
    for load in raw:
        load.start()
    loads = [
        pltpu.make_async_copy(
            emb_hbm.at[:, pl.ds(pl.multiple_of(f * share, 128), share)], emb, load_sem.at[0]
        ),
        pltpu.make_async_copy(conv_hbm.at[0], convw.at[0], load_sem.at[1]),
        pltpu.make_async_copy(conv_hbm.at[1], convw.at[1], load_sem.at[2]),
        pltpu.make_async_copy(conv_hbm.at[2], convw.at[2], load_sem.at[3]),
        pltpu.make_async_copy(time_hbm, timew, load_sem.at[4]),
        pltpu.make_async_copy(o_hbm, ow, load_sem.at[5]),
    ]
    for load in loads:
        load.start()

    barrier = pltpu.get_barrier_semaphore()
    for k in (1, 2, 3):
        pf, pr = peer(k)
        pl.semaphore_signal(barrier, inc=1, device_id=(asset, pf, pr), device_id_type=MESH)
    for other_asset in (sibling, above):
        pl.semaphore_signal(barrier, inc=1, device_id=(other_asset, f, r), device_id_type=MESH)
    pl.semaphore_wait(barrier, 5)

    def latent_copy(k, slot):
        return remote(latent_ref.at[0], latbuf.at[slot], lat_send.at[k], lat_recv.at[k], k)

    local_latent = pltpu.make_async_copy(latent_ref.at[0], latbuf.at[r], load_sem.at[7])

    def relay_copy(i):
        return remote(latent_ref.at[0, i], relay.at[i], rl_send.at[i], rl_recv.at[i], 2)

    def relay_forward(i, slot):
        return remote(relay.at[i], latbuf.at[slot, i], rl_send.at[i], rl_recv.at[i], 1)

    @pl.when(f == r)
    def _():
        latent_copy(2, r).start()
        local_latent.start()

    @pl.when(f != r)
    def _():
        for i in range(band):
            relay_copy(i).start()
        latent_copy(1, r).start()

    dec_copy = remote(dec_ref.at[0], decoth, dec_send, dec_recv, 2)
    dec_copy.start()

    dec_own = dec_ref[0].astype(jnp.float32).reshape(cells, dec_channels)
    dec_sum = jnp.sum(dec_own, axis=0, keepdims=True)
    dec_square = jnp.sum(dec_own * dec_own, axis=0, keepdims=True)
    stats[0] = jnp.concatenate(
        [dec_sum, dec_square, jnp.zeros((6, dec_channels), jnp.float32)], axis=0
    )
    stat_copies = [
        remote(stats.at[0], stats.at[k], st_send.at[k], st_recv.at[k], k) for k in (1, 2, 3)
    ]
    for copy in stat_copies:
        copy.start()

    for load in raw:
        load.wait()
    for i in range(3):
        for target in range(4):
            wsend[target, i] = wraw[i, :, target * rows : (target + 1) * rows]
    local_weight = pltpu.make_async_copy(
        wsend.at[me], wg.at[:, pl.ds(pl.multiple_of(me * rows, 16), rows), :], load_sem.at[6]
    )
    local_weight.start()

    entries = emb.shape[0] // 3
    lanes = lax.broadcasted_iota(jnp.int32, (8, 3 * entries), 1)
    second_piece = lanes >= entries
    third_piece = lanes >= 2 * entries
    entry_at = jnp.where(
        third_piece, lanes - 2 * entries, jnp.where(second_piece, lanes - entries, lanes)
    )
    is_sine = entry_at >= entries // 2
    order = jnp.where(is_sine, entry_at - entries // 2, entry_at).astype(jnp.float32)
    freqs = jnp.exp(-math.log(10000.0) * order / (entries // 2))
    value = jnp.where(
        third_piece,
        camera_ref[r, 1].astype(jnp.float32),
        jnp.where(
            second_piece, camera_ref[r, 0].astype(jnp.float32), time_ref[0].astype(jnp.float32)
        ),
    )
    angles = value * freqs
    feats = silu(jnp.where(is_sine, jnp.sin(angles), jnp.cos(angles))).astype(jnp.bfloat16)
    loads[0].wait()
    cond = jnp.dot(feats, emb[...], preferred_element_type=jnp.float32)[0:1]

    xcat[0:stride, :] = jnp.zeros((stride, 3 * channels), jnp.bfloat16)
    xcat[5 * stride : 6 * stride, :] = jnp.zeros((stride, 3 * channels), jnp.bfloat16)

    @pl.when(f == r)
    def _():
        local_latent.wait()
        for i in range(band):
            relay_copy(i).wait_recv()
            relay_forward(i, r).start()
        latent_copy(1, 1 - r).wait_recv()

    @pl.when(f != r)
    def _():
        latent_copy(2, r).wait_recv()
        for i in range(band):
            relay_forward(i, 1 - r).wait_recv()

    def source_rows(k, which):
        pf, pr = peer(k)
        source = 2 * pf + pr
        return pl.ds(pl.multiple_of(source * rows + which * quarter, 16), quarter)

    def weight_copy(k):
        pf, pr = peer(k)
        target = 2 * pf + pr
        mine = pl.ds(pl.multiple_of(part * quarter, 16), quarter)
        there = pl.ds(pl.multiple_of(me * rows + part * quarter, 16), quarter)
        return remote(
            wsend.at[target, :, mine, :], wg.at[:, there, :], w_send.at[k], w_recv.at[k], k
        )

    def weight_arrival(k):
        where = wg.at[:, source_rows(k, part), :]
        return remote(where, where, w_send.at[k], w_recv.at[k], k)

    def weight_pass(k, which, send, recv, other_asset):
        where = wg.at[:, source_rows(k, which), :]
        return pltpu.make_async_remote_copy(
            src_ref=where,
            dst_ref=where,
            send_sem=send,
            recv_sem=recv,
            device_id=(other_asset, f, r),
            device_id_type=MESH,
        )

    def weight_up(k, which):
        return weight_pass(k, which, zw_send.at[k], zw_recv.at[k], above)

    def weight_side(k, j, which):
        return weight_pass(k, which, fw_send.at[j, k], fw_recv.at[j, k], sibling)

    for k in (3, 1, 2):
        weight_copy(k).start()

    total = jnp.zeros((1, channels), jnp.float32)
    square = jnp.zeros((1, channels), jnp.float32)
    for i in range(2 * band):
        x = latbuf[i // band, i % band].astype(jnp.float32)
        total = total + jnp.sum(x, axis=0, keepdims=True)
        square = square + jnp.sum(x * x, axis=0, keepdims=True)
    sums = jnp.concatenate([total, square, jnp.zeros((6, channels), jnp.float32)], axis=0)
    number = float(2 * cells * (channels // G))
    mean, scale = group_norm_terms(sums, number, channels)
    for i in range(2 * band):
        x = latbuf[i // band, i % band].astype(jnp.float32)
        act = silu((x - mean) * scale * gain_ref[...].reshape(1, -1) + shift_ref[...].reshape(1, -1))
        padded = jnp.concatenate([act, jnp.zeros((8, channels), jnp.float32)], axis=0)
        at = slice((i + 1) * stride, (i + 2) * stride)
        xcat[at, 0:channels] = pltpu.roll(padded, 1, 0).astype(jnp.bfloat16)
        xcat[at, channels : 2 * channels] = padded.astype(jnp.bfloat16)
        xcat[at, 2 * channels :] = pltpu.roll(padded, stride - 1, 0).astype(jnp.bfloat16)

    def spatial_copy(k, n, frame, start, size):
        where = spat.at[frame, :, pl.ds(pl.multiple_of(start, 128), size)]
        return remote(where, where, sp_send.at[n, k], sp_recv.at[n, k], k)

    def entry(n):
        return 1 if n == 1 else 2

    def pass_on(n):
        start, size = CHUNKS[n]
        pf, pr = peer(entry(n))
        spatial_copy(entry(n), n, pr, pf * share + start, size).wait_recv()
        where = spat.at[pr, :, pl.ds(pl.multiple_of(pf * share + start, 128), size)]
        remote(where, where, sp_send.at[n, 3], sp_recv.at[n, 3], 3 - entry(n)).start()

    for load in loads[1:4]:
        load.wait()
    for n, (start, size) in enumerate(CHUNKS):

        def tap(a, acc):
            lhs = xcat[pl.ds(pl.multiple_of(a * stride, 16), 2 * band * stride), :]
            rhs = convw[a, :, :, start : start + size].reshape(3 * channels, size)
            return acc + jnp.dot(lhs, rhs, preferred_element_type=jnp.float32)

        acc = lax.fori_loop(0, 3, tap, jnp.zeros((2 * band * stride, size), jnp.float32))
        acc = acc.reshape(2 * band, stride, size)[:, :width]
        column = pl.ds(pl.multiple_of(f * share + start, 128), size)
        res = latbuf[:, :, :, column].astype(jnp.float32).reshape(2 * band, width, size)
        new = res + acc + cond[:, start : start + size].reshape(1, 1, size)
        spat[r, :, column] = new.reshape(2 * cells, size).astype(jnp.bfloat16)
        for k in (1, 2):
            spatial_copy(k, n, r, f * share + start, size).start()
        if n == 1:
            for k in (3, 1, 2):
                weight_arrival(k).wait_recv()
                weight_up(k, part).start()
                weight_side(k, 0, part).start()

    pass_on(0)
    pass_on(1)

    dec_copy.wait_recv()
    for copy in stat_copies:
        copy.wait_recv()
    dec_total = stats[0] + stats[1] + stats[2] + stats[3]
    dec_number = float(4 * cells * (dec_channels // G))
    dmean, dscale = group_norm_terms(dec_total, dec_number, dec_channels)

    def dec_act(x):
        return silu((x - dmean) * dscale * dgain_ref[...].reshape(1, -1) + dshift_ref[...].reshape(1, -1)).astype(jnp.bfloat16)

    dec_values = dec_ref[0].astype(jnp.float32).reshape(cells, dec_channels)
    middle = dec_act(dec_values)
    around = dec_act(decoth[...].astype(jnp.float32).reshape(cells, dec_channels))
    loads[4].wait()
    temporal = jnp.dot(around, timew[0], preferred_element_type=jnp.float32)
    temporal = temporal + jnp.dot(middle, timew[1], preferred_element_type=jnp.float32)
    temporal = temporal + jnp.dot(around, timew[2], preferred_element_type=jnp.float32)
    dec_out_ref[0] = (
        (dec_values + temporal).reshape(band, width, dec_channels).astype(jnp.bfloat16)
    )

    pass_on(2)

    head_size = channels // HEADS
    lane = lax.broadcasted_iota(jnp.int32, (rows, 128), 0)
    low = lax.broadcasted_iota(jnp.int32, (rows, 128), 1) * head_size
    member = jnp.where((lane >= low) & (lane < low + head_size), 1.0, 0.0).astype(jnp.bfloat16)
    loads[5].wait()
    local_weight.wait()
    for k in (3, 1, 2):
        weight_up(k, part_above).wait_recv()
        weight_side(k, 1, part_above).start()
    for n, (start, size) in enumerate(CHUNKS):
        for k in (3 - entry(n), 3):
            pf, pr = peer(k)
            spatial_copy(k, n, pr, pf * share + start, size).wait_recv()
    for k in (3, 1, 2):
        weight_side(k, 0, 2 * plane + 1 - core).wait_recv()
        weight_side(k, 1, 2 * (1 - plane) + 1 - core).wait_recv()

    def share_of(which):
        where = pl.ds(pl.multiple_of(which * cells, 16), cells)
        tokens = jnp.concatenate([spat[0, where, :], spat[1, where, :]], axis=0).astype(jnp.float32)
        mean = jnp.mean(tokens, axis=-1, keepdims=True)
        square = jnp.mean(tokens * tokens, axis=-1, keepdims=True)
        scale = lax.rsqrt(square - mean * mean + EPSILON)
        normal = ((tokens - mean) * scale * ln_ref[...].reshape(1, -1)).astype(jnp.bfloat16)
        q, k, v = [
            jnp.dot(normal, wg[i], preferred_element_type=jnp.float32)
            .astype(jnp.bfloat16)
            .astype(jnp.float32)
            for i in range(3)
        ]
        high, rest = [], []
        for a in range(2):
            for b in range(2):
                product = q[a * cells : (a + 1) * cells] * k[b * cells : (b + 1) * cells]
                top = product.astype(jnp.bfloat16)
                high.append(top)
                rest.append((product - top.astype(jnp.float32)).astype(jnp.bfloat16))
        dots = jnp.dot(
            jnp.concatenate(high + rest, axis=0), member, preferred_element_type=jnp.float32
        )
        scores = (dots[: 4 * cells] + dots[4 * cells :]) * (1.0 / math.sqrt(head_size))
        weights = jnp.exp(scores)
        probs = []
        for a in range(2):
            pair = [weights[(2 * a + b) * cells : (2 * a + b + 1) * cells] for b in range(2)]
            bottom = pair[0] + pair[1]
            probs += [(one / bottom).astype(jnp.bfloat16) for one in pair]
        spread = lax.dot_general(
            jnp.concatenate(probs, axis=0),
            member,
            (((1,), (1,)), ((), ())),
            preferred_element_type=jnp.float32,
        )
        mixed = [
            spread[2 * a * cells : (2 * a + 1) * cells] * v[:cells]
            + spread[(2 * a + 1) * cells : (2 * a + 2) * cells] * v[cells:]
            for a in range(2)
        ]
        mixed = jnp.concatenate(mixed, axis=0).astype(jnp.bfloat16)
        return jnp.dot(mixed, ow[...], preferred_element_type=jnp.float32)

    middle_channel = channels // 2
    left = slice(0, middle_channel)
    right = slice(middle_channel, channels)

    def result_copy(i):
        slot, k, side = ((3, 1, 0), (3, 2, 1), (1, 1, 0), (1, 1, 1), (2, 2, 0), (2, 2, 1))[i]
        columns = pl.ds(side * middle_channel, middle_channel)
        return remote(
            psend.at[slot, :, columns], precv.at[slot, :, columns], rs_send.at[i], rs_recv.at[i], k
        )

    other = share_of(1 - r)
    far = jnp.where(f == 0, other[cells:], other[:cells])
    near = jnp.where(f == 0, other[:cells], other[cells:])
    psend[3] = far.astype(jnp.bfloat16)
    result_copy(1).start()
    result_copy(0).start()
    psend[1, :, left] = near[:, left].astype(jnp.bfloat16)
    result_copy(2).start()
    own = share_of(r)
    second = jnp.where(f == 0, own[cells:], own[:cells])
    mine = jnp.where(f == 0, own[:cells], own[cells:])
    psend[2, :, right] = second[:, right].astype(jnp.bfloat16)
    result_copy(5).start()
    result_copy(0).wait_recv()
    psend[2, :, left] = (second[:, left] + precv[3, :, left].astype(jnp.float32)).astype(
        jnp.bfloat16
    )
    result_copy(4).start()
    result_copy(1).wait_recv()
    psend[1, :, right] = (near[:, right] + precv[3, :, right].astype(jnp.float32)).astype(
        jnp.bfloat16
    )
    result_copy(3).start()
    where = pl.ds(pl.multiple_of(r * cells, 16), cells)
    result = spat[f, where, :].astype(jnp.float32) + mine
    for i in (2, 3, 4, 5):
        result_copy(i).wait_recv()
    result = result + precv[1].astype(jnp.float32) + precv[2].astype(jnp.float32)
    out_ref[0] = result.reshape(band, width, channels).astype(jnp.bfloat16)

    @pl.when(f == r)
    def _():
        latent_copy(2, r).wait_send()
        for i in range(band):
            relay_forward(i, r).wait_send()

    @pl.when(f != r)
    def _():
        for i in range(band):
            relay_copy(i).wait_send()
        latent_copy(1, r).wait_send()

    dec_copy.wait_send()
    for copy in stat_copies:
        copy.wait_send()
    for i in range(6):
        result_copy(i).wait_send()
    for k in (1, 2, 3):
        weight_copy(k).wait_send()
        weight_up(k, part).wait_send()
        weight_side(k, 0, part).wait_send()
        weight_side(k, 1, part_above).wait_send()
        for n, (start, size) in enumerate(CHUNKS):
            spatial_copy(k, n, r, f * share + start, size).wait_send()


def place(unet_ref, dec_ref, unet_out, dec_out, sem):
    copies = [
        pltpu.make_async_copy(unet_ref, unet_out, sem.at[0]),
        pltpu.make_async_copy(dec_ref, dec_out, sem.at[1]),
    ]
    for copy in copies:
        copy.start()
    for copy in copies:
        copy.wait()


def fused(
    latent,
    timestep,
    camera,
    dec_feat,
    norm_gain,
    norm_shift,
    emb_weight,
    conv_weight,
    ln_gain,
    q_weight,
    k_weight,
    v_weight,
    o_weight,
    dec_gain,
    dec_shift,
    time_weight,
):
    _, band, width, channels = latent.shape
    share = conv_weight.shape[3]
    rows = q_weight.shape[0]
    cells = band * width
    dec_channels = dec_feat.shape[3]
    vmem = pl.BlockSpec(memory_space=pltpu.VMEM)
    smem = pl.BlockSpec(memory_space=pltpu.SMEM)
    hbm = pl.BlockSpec(memory_space=pl.ANY)
    dma = pltpu.SemaphoreType.DMA
    bf16, f32 = jnp.bfloat16, jnp.float32
    unet, dec = pl.pallas_call(
        kernel,
        out_shape=(
            jax.ShapeDtypeStruct(latent.shape, bf16),
            jax.ShapeDtypeStruct(dec_feat.shape, bf16),
        ),
        in_specs=[vmem] * 2 + [smem] * 2 + [vmem] * 5 + [hbm] * 7,
        out_specs=(vmem, vmem),
        scratch_shapes=[
            pltpu.VMEM((3, rows, channels), bf16),
            pltpu.VMEM((4, 3, rows, rows), bf16),
            pltpu.VMEM((band, width, channels), bf16),
            pltpu.VMEM(conv_weight.shape, bf16),
            pltpu.VMEM((emb_weight.shape[0], share), bf16),
            pltpu.VMEM(o_weight.shape, bf16),
            pltpu.VMEM(time_weight.shape, bf16),
            pltpu.VMEM((2, band, width, channels), bf16),
            pltpu.VMEM((6 * (width + 8), 3 * channels), bf16),
            pltpu.VMEM((2, 2 * cells, channels), bf16),
            pltpu.VMEM((3, channels, rows), bf16),
            pltpu.VMEM((band, width, dec_channels), bf16),
            pltpu.VMEM((4, 8, dec_channels), f32),
            pltpu.VMEM((4, cells, channels), bf16),
            pltpu.VMEM((4, cells, channels), bf16),
            dma((11,)),
            dma((4,)),
            dma((4,)),
            dma,
            dma,
            dma((4,)),
            dma((4,)),
            dma((4,)),
            dma((4,)),
            dma((4,)),
            dma((4,)),
            dma((2, 4)),
            dma((2, 4)),
            dma((band,)),
            dma((band,)),
            dma((3, 4)),
            dma((3, 4)),
            dma((6,)),
            dma((6,)),
        ],
        compiler_params=pltpu.CompilerParams(
            collective_id=0, has_side_effects=True, vmem_limit_bytes=60 * 1024 * 1024
        ),
        name="denoise",
    )(
        latent,
        dec_feat,
        timestep,
        camera,
        norm_gain,
        norm_shift,
        ln_gain,
        dec_gain,
        dec_shift,
        emb_weight,
        conv_weight,
        q_weight,
        k_weight,
        v_weight,
        o_weight,
        time_weight,
    )
    return pl.pallas_call(
        place,
        out_shape=(
            jax.ShapeDtypeStruct(latent.shape, bf16),
            jax.ShapeDtypeStruct(dec_feat.shape, bf16),
        ),
        in_specs=[vmem, vmem],
        out_specs=(hbm, hbm),
        scratch_shapes=[dma((2,))],
        name="place",
    )(unet, dec)


def solution(mesh):
    in_specs = (
        P(("asset", "frame"), "row", None, None),
        P("asset"),
        P("asset", None),
        P(("asset", "frame"), "row", None, None),
        P(),
        P(),
        P(),
        P(None, None, None, "frame"),
        P(),
        P(("frame", "row"), None),
        P(("frame", "row"), None),
        P(("frame", "row"), None),
        P(("frame", "row"), None),
        P(),
        P(),
        P(),
    )
    out_specs = (P(("asset", "frame"), "row", None, None), P(("asset", "frame"), "row", None, None))
    sizes = dict(mesh.shape)
    small = sizes["frame"] == 2 and sizes["row"] == 2 and sizes["asset"] % 4 == 0
    return jax.shard_map(fused if small else body, mesh=mesh, in_specs=in_specs, out_specs=out_specs, check_vma=False)
```
